256 devices in a mesh: slab: 64 (over y, z, x_hi), term: 4 (over x_lo, core).
Axes of the slice: x: 4 (x_hi: 2, x_lo: 2; x = x_hi * 2 + x_lo), y: 4, z: 8, core: 2. Of those that a mesh axis runs over, the one named last changes fastest.
Arguments:
- right_side: float32 [84, 128, 128, 128], P('term', 'slab'), may hold values from -24 to 24
- mean_cond: float32 [128, 128, 128], P('slab', 'term'), may hold values from 2 to 4
- cond_terms: float32 [6, 128, 128, 128], P(None, 'slab', 'term'), may hold values from -0.3 to 0.3
Outputs:
- solution: float32 [84, 128, 128, 128], P('term', 'slab')
- residual: float32 [84, 128, 128, 128], P('term', 'slab')
The draws below stay inside these ranges and needn't reach their ends.
All inputs are finite; a program needn't handle non-finite values.
Results may differ from the reference program's by a relative error of at most 0.00013.
Values sent between devices are 32-bit elements; how exact they have to be, the bound alone decides.
No kernel may reach another device: no remote copies, remote signals or barrier semaphores. Data moves between devices by JAX's collectives and lax.ppermute only.
A program may use at most 64 MiB of HBM per device.

```python
import math
import jax
import jax.numpy as jnp
from jax import lax

DIM = 6
DEG = 3
P_SIZE = 84
ITERS = 2
NX = 128
NY = 128
NZ = 128


def block_levels(rng, shape, split, least, high):
    def one(dim, shards_of):
        draws = jax.random.uniform(jax.random.fold_in(jax.random.fold_in(rng, 6), dim), (shards_of,), jnp.float32, least / len(split), high / len(split))
        return jnp.repeat(jnp.exp(draws), shape[dim] // shards_of).reshape((-1,) + (1,) * (len(shape) - dim - 1))

    gain = one(*split[0])
    for cut in split[1:]:
        gain = gain * one(*cut)
    return gain


def bell_draw(own_key, extent, scale, bound, cuts=(), kind=jnp.bfloat16):
    drawn = scale * jax.random.normal(own_key, extent, jnp.float32)
    if cuts:
        drawn = drawn * block_levels(own_key, extent, cuts, -0.22, 0.18)
    return jnp.clip(drawn, -bound, bound).astype(kind)


def setup_inputs(seed: int = 0) -> dict:
    splits = jax.random.split(jax.random.key(seed), 4)
    right_side = bell_draw(splits[0], (P_SIZE, NZ, NY, NX), 4.0, 24.0, ((0, 4), (1, 64)), jnp.float32)
    mean_cond = jnp.clip(2.0 + 2.0 * jax.random.uniform(splits[1], (NZ, NY, NX), jnp.float32) ** block_levels(splits[1], (NZ, NY, NX), ((0, 64), (1, 4)), -0.2, 0.2), 2.0, 4.0)
    cond_terms = jnp.clip(jax.random.uniform(splits[2], (DIM, NZ, NY, NX), jnp.float32, -0.3, 0.3) * block_levels(splits[2], (DIM, NZ, NY, NX), ((1, 64), (2, 4)), -0.4, 0.0), -0.3, 0.3)
    return {"right_side": right_side, "mean_cond": mean_cond, "cond_terms": cond_terms}


lower_edge = 2.0
upper_edge = 72.0

def compositions(degree_sum, slots_left):
    if slots_left == 1:
        return [[degree_sum]]
    listing = []
    for leading in range(degree_sum, -1, -1):
        for remainder in compositions(degree_sum - leading, slots_left - 1):
            listing.append([leading] + remainder)
    return listing

def galerkin_tables(variables, degree):
    indices = []
    for degree_level in range(degree + 1):
        indices.extend(compositions(degree_level, variables))
    count = len(indices)
    tables = []
    for variable in range(variables):
        rows_list = []
        for row in range(count):
            first = indices[row]
            entries = []
            for col in range(count):
                second = indices[col]
                agreeing = all((first[m] == second[m] for m in range(variables) if m != variable))
                value = 0.0
                if agreeing and abs(first[variable] - second[variable]) == 1:
                    higher = max(first[variable], second[variable])
                    value = higher / math.sqrt(4.0 * higher * higher - 1.0)
                entries.append(value)
            rows_list.append(entries)
        tables.append(rows_list)
    return tables

def laplace(extended, field):
    beside = extended[:, 2:, 1:-1, 1:-1] + extended[:, :-2, 1:-1, 1:-1]
    beside = beside + extended[:, 1:-1, 2:, 1:-1] + extended[:, 1:-1, :-2, 1:-1]
    beside = beside + extended[:, 1:-1, 1:-1, 2:] + extended[:, 1:-1, 1:-1, :-2]
    return 6.0 * field - beside

def coupling(lap_field, mean_cond, cond_terms, tables):
    flat = lap_field.reshape(lap_field.shape[0], -1)
    result = mean_cond.reshape(1, -1) * flat
    terms_flat = cond_terms.reshape(cond_terms.shape[0], -1)
    for variable in range(cond_terms.shape[0]):
        mixed = jnp.dot(tables[variable], flat, precision=lax.Precision.HIGHEST, preferred_element_type=jnp.float32)
        result = result + terms_flat[variable][None, :] * mixed
    return result.reshape(lap_field.shape)

def chebyshev(right_side, apply_operator):
    center_value = 0.5 * (upper_edge + lower_edge)
    half_width = 0.5 * (upper_edge - lower_edge)
    sigma_value = center_value / half_width
    rho_now = 1.0 / sigma_value
    residual = right_side
    direction = right_side / center_value
    solution = jnp.zeros_like(right_side)
    for iteration in range(ITERS):
        solution = solution + direction
        residual = residual - apply_operator(direction)
        rho_next = 1.0 / (2.0 * sigma_value - rho_now)
        if iteration + 1 < ITERS:
            direction = rho_next * rho_now * direction + 2.0 * rho_next / half_width * residual
        rho_now = rho_next
    return (solution, residual)

def reference(right_side, mean_cond, cond_terms):
    tables = jnp.asarray(galerkin_tables(DIM, DEG), jnp.float32)

    def apply_operator(field):
        extended = jnp.pad(field, ((0, 0), (1, 1), (1, 1), (1, 1)))
        lap_field = laplace(extended, field)

        def per_plane(pieces):
            return coupling(pieces[0], pieces[1], pieces[2], tables)
        planes = lax.map(per_plane, (jnp.moveaxis(lap_field, 1, 0), mean_cond, jnp.moveaxis(cond_terms, 1, 0)))
        return jnp.moveaxis(planes, 0, 1)
    solution, residual = chebyshev(right_side, apply_operator)
    return (solution, residual)
```

```python
import math

import jax
import jax.numpy as jnp
from jax import lax
from jax.experimental import pallas as pl
from jax.experimental.pallas import tpu as pltpu
from jax.sharding import Mesh, PartitionSpec as P

DIM = 6
DEG = 3
LOWER = 2.0
UPPER = 72.0

TERMS = 84
T4 = 21
ROWS = 16
LANES = 128
F32 = jnp.float32
VMEM_BYTES = 48 * 1024 * 1024


def compositions(degree_sum, slots_left):
    if slots_left == 1:
        return [[degree_sum]]
    listing = []
    for leading in range(degree_sum, -1, -1):
        for remainder in compositions(degree_sum - leading, slots_left - 1):
            listing.append([leading] + remainder)
    return listing


def couplings(variables, degree):
    indices = []
    for level in range(degree + 1):
        indices.extend(compositions(level, variables))
    place = {tuple(m): n for n, m in enumerate(indices)}
    result = []
    for first in indices:
        rows = []
        for k in range(variables):
            found = []
            for step in (-1, 1):
                other = list(first)
                other[k] += step
                j = place.get(tuple(other))
                if j is not None:
                    n = max(first[k], other[k])
                    found.append((j, n / math.sqrt(4.0 * n * n - 1.0)))
            if found:
                rows.append((k, found))
        result.append(rows)
    return result


def scalars():
    center = 0.5 * (UPPER + LOWER)
    half = 0.5 * (UPPER - LOWER)
    sigma = center / half
    rho0 = 1.0 / sigma
    rho1 = 1.0 / (2.0 * sigma - rho0)
    keep = (1.0 + rho1 * rho0) / center + 2.0 * rho1 / half
    mix = -2.0 * rho1 / half / center
    return keep, mix


COUPLE = couplings(DIM, DEG)
KEEP, MIX = scalars()

ANY = pl.BlockSpec(memory_space=pl.ANY)
SMEM = pl.BlockSpec(memory_space=pltpu.SMEM)


def pack_kernel(s_ref, x_ref, *refs):
    outs = refs[:8]
    xv, hv, sem_in, sem_main, sem_halo = refs[8:]
    plane, band = s_ref[0], s_ref[1]
    load = pltpu.make_async_copy(x_ref.at[:, plane], xv, sem_in)
    load.start()
    load.wait()
    copies = []
    for k in range(8):
        d = jnp.bitwise_xor(band, k)
        start = pl.multiple_of(d * ROWS, ROWS)
        c = pltpu.make_async_copy(
            xv.at[:, pl.ds(start, ROWS), :], outs[k].at[pl.ds(0, T4)], sem_main.at[k]
        )
        c.start()
        copies.append(c)
        above = jnp.maximum(d * ROWS - 1, 0)
        below = jnp.minimum(d * ROWS + ROWS, 127)
        for j in range(T4):
            up = xv[j, pl.ds(above, 1), :]
            dn = xv[j, pl.ds(below, 1), :]
            up = jnp.where(d == 0, jnp.zeros_like(up), up)
            dn = jnp.where(d == 7, jnp.zeros_like(dn), dn)
            a, b = j, 24 + j
            hv[k, a // 16, pl.ds(a % 16, 1), :] = up
            hv[k, b // 16, pl.ds(b % 16, 1), :] = dn
        c = pltpu.make_async_copy(hv.at[k], outs[k].at[pl.ds(T4, 3)], sem_halo.at[k])
        c.start()
        copies.append(c)
    for c in copies:
        c.wait()


def pack(info, x):
    return pl.pallas_call(
        pack_kernel,
        out_shape=[jax.ShapeDtypeStruct((24, ROWS, LANES), F32)] * 8,
        in_specs=[SMEM, ANY],
        out_specs=[ANY] * 8,
        scratch_shapes=[
            pltpu.VMEM((T4, 128, LANES), F32),
            pltpu.VMEM((8, 3, ROWS, LANES), F32),
            pltpu.SemaphoreType.DMA,
            pltpu.SemaphoreType.DMA((8,)),
            pltpu.SemaphoreType.DMA((8,)),
        ],
        compiler_params=pltpu.CompilerParams(vmem_limit_bytes=VMEM_BYTES),
        name="pack",
    )(info, x)


def start_all(pairs, sems):
    copies = [pltpu.make_async_copy(a, b, sems.at[n]) for n, (a, b) in enumerate(pairs)]
    for c in copies:
        c.start()
    return copies


def laplace_plane(v_ref, lap, p, up_row, dn_row):
    row = lax.broadcasted_iota(jnp.int32, (ROWS, LANES), 0)
    lane = lax.broadcasted_iota(jnp.int32, (ROWS, LANES), 1)
    first_row, last_row = row == 0, row == ROWS - 1
    first_lane, last_lane = lane == 0, lane == LANES - 1

    def group(t, carry):
        for jj in range(T4):
            j = t * T4 + jj
            c = v_ref[j, p + 1]
            dn = jnp.where(last_row, dn_row(t, p, jj), pltpu.roll(c, ROWS - 1, 0))
            up = jnp.where(first_row, up_row(t, p, jj), pltpu.roll(c, 1, 0))
            right = jnp.where(last_lane, 0.0, pltpu.roll(c, LANES - 1, 1))
            left = jnp.where(first_lane, 0.0, pltpu.roll(c, 1, 1))
            beside = v_ref[j, p + 2] + v_ref[j, p]
            beside = beside + dn + up
            beside = beside + right + left
            lap[j] = 6.0 * c - beside
        return carry

    lax.fori_loop(0, 4, group, 0)


def coupled(lap, cond, p, i):
    acc = cond[0, p] * lap[i]
    for k, found in COUPLE[i]:
        mixed = None
        for j, weight in found:
            part = weight * lap[j]
            mixed = part if mixed is None else mixed + part
        acc = acc + cond[k + 1, p] * mixed
    return acc


def place_of(s_ref, k):
    h = jnp.bitwise_xor(s_ref[0], k >> 2)
    t = jnp.bitwise_xor(s_ref[1], k & 3)
    return h, t


def conductivity_pairs(s_ref, near, far, cond):
    odd = s_ref[2]
    return [
        (near, cond.at[:, pl.ds(2 * odd, 2)]),
        (far, cond.at[:, pl.ds(2 * (1 - odd), 2)]),
    ]


def first_kernel(s_ref, *refs):
    outer, inner = refs[0:8], refs[8:16]
    zlo, zhi, near, far = refs[16:20]
    outs = refs[20:28]
    z0, z3, y0, y15 = refs[28:32]
    v, halo, lap, out, cond, y0v, y15v, sem_v, sem_h, sem_o, sem_e = refs[32:]
    h = s_ref[0]

    pairs, halos = [], []
    for k in range(8):
        hk, tk = place_of(s_ref, k)
        terms = pl.ds(tk * T4, T4)
        pairs.append((outer[k].at[pl.ds(0, T4)], v.at[terms, 3 * hk + 1]))
        pairs.append((inner[k].at[pl.ds(0, T4)], v.at[terms, 2 + hk]))
        halos.append((outer[k].at[pl.ds(T4, 3)], halo.at[tk, 3 * hk]))
        halos.append((inner[k].at[pl.ds(T4, 3)], halo.at[tk, 1 + hk]))
    for k in range(4):
        tk = jnp.bitwise_xor(s_ref[1], k)
        terms = pl.ds(tk * T4, T4)
        pairs.append((zlo.at[pl.ds(k * T4, T4)], v.at[terms, 5 * (1 - h)]))
        pairs.append((zhi.at[pl.ds(k * T4, T4)], v.at[terms, 5 * h]))
    halos += conductivity_pairs(s_ref, near, far, cond)
    loads = start_all(pairs, sem_v) + start_all(halos, sem_h)
    for c in loads:
        c.wait()

    def up_row(t, p, jj):
        return halo[t, p, jj // 16, pl.ds(jj % 16, 1), :]

    def dn_row(t, p, jj):
        return halo[t, p, (24 + jj) // 16, pl.ds((24 + jj) % 16, 1), :]

    def sends(group):
        result = []
        for kk in range(4):
            k = group * 4 + kk
            hk, tk = place_of(s_ref, k)
            result.append(
                pltpu.make_async_copy(
                    out.at[pl.ds(tk * T4, T4), pl.ds(2 * hk, 2)], outs[k], sem_o.at[k]
                )
            )
        return result

    def plane_step(s, carry):
        p = 2 * jnp.bitwise_xor(h, s // 2) + s % 2
        laplace_plane(v, lap, p, up_row, dn_row)
        for i in range(TERMS):
            value = KEEP * v[i, p + 1] + MIX * coupled(lap, cond, p, i)
            out[i, p] = value
            y0v[i // T4, p, pl.ds(i % T4, 1), :] = value[0:1]
            y15v[i // T4, p, pl.ds(i % T4, 1), :] = value[ROWS - 1 : ROWS]
        for group in range(2):

            @pl.when(s == 2 * group + 1)
            def _():
                for c in sends(group):
                    c.start()

        return carry

    for t in range(4):
        for n in range(4):
            y0v[t, n, T4:24, :] = jnp.zeros((24 - T4, LANES), F32)
            y15v[t, n, T4:24, :] = jnp.zeros((24 - T4, LANES), F32)
    lax.fori_loop(0, 4, plane_step, 0)
    edges = start_all(
        [(out.at[:, 0], z0), (out.at[:, 3], z3), (y0v, y0), (y15v, y15)], sem_e
    )
    for c in edges + sends(0) + sends(1):
        c.wait()


def second_kernel(s_ref, *refs):
    outer, inner, sol = refs[0:8], refs[8:16], refs[16:24]
    below, above, yup, ydn, near, far = refs[24:30]
    outs = refs[30:38]
    v, r, lap, out, cond, upv, dnv, sem_v, sem_e, sem_o = refs[38:]
    h = s_ref[0]

    pairs = []
    for k in range(8):
        hk, tk = place_of(s_ref, k)
        terms = pl.ds(tk * T4, T4)
        pairs.append((sol[k], v.at[terms, pl.ds(2 * hk + 1, 2)]))
        pairs.append((outer[k].at[pl.ds(0, T4)], r.at[terms, 3 * hk]))
        pairs.append((inner[k].at[pl.ds(0, T4)], r.at[terms, 1 + hk]))
    edges = [(below, v.at[:, 0]), (above, v.at[:, 5]), (yup, upv), (ydn, dnv)]
    edges += conductivity_pairs(s_ref, near, far, cond)
    loads = start_all(pairs, sem_v) + start_all(edges, sem_e)
    for c in loads:
        c.wait()

    def up_row(t, p, jj):
        return upv[t, p, pl.ds(jj, 1), :]

    def dn_row(t, p, jj):
        return dnv[t, p, pl.ds(jj, 1), :]

    def sends(group):
        result = []
        for kk in range(4):
            k = group * 4 + kk
            hk, tk = place_of(s_ref, k)
            result.append(
                pltpu.make_async_copy(
                    out.at[pl.ds(tk * T4, T4), pl.ds(2 * hk, 2)], outs[k], sem_o.at[k]
                )
            )
        return result

    def plane_step(s, carry):
        p = 2 * jnp.bitwise_xor(h, s // 2) + s % 2
        laplace_plane(v, lap, p, up_row, dn_row)
        for i in range(TERMS):
            out[i, p] = r[i, p] - coupled(lap, cond, p, i)
        for group in range(2):

            @pl.when(s == 2 * group + 1)
            def _():
                for c in sends(group):
                    c.start()

        return carry

    lax.fori_loop(0, 4, plane_step, 0)
    for c in sends(0) + sends(1):
        c.wait()


PIECE = jax.ShapeDtypeStruct((T4, 2, ROWS, LANES), F32)
FACE = jax.ShapeDtypeStruct((TERMS, ROWS, LANES), F32)
EDGE = jax.ShapeDtypeStruct((4, 4, 24, LANES), F32)


def dma(count):
    return pltpu.SemaphoreType.DMA((count,))


def first(info, *arrays):
    return pl.pallas_call(
        first_kernel,
        out_shape=[PIECE] * 8 + [FACE] * 2 + [EDGE] * 2,
        in_specs=[SMEM] + [ANY] * 20,
        out_specs=[ANY] * 12,
        scratch_shapes=[
            pltpu.VMEM((TERMS, 6, ROWS, LANES), F32),
            pltpu.VMEM((4, 4, 3, ROWS, LANES), F32),
            pltpu.VMEM((TERMS, ROWS, LANES), F32),
            pltpu.VMEM((TERMS, 4, ROWS, LANES), F32),
            pltpu.VMEM((DIM + 1, 4, ROWS, LANES), F32),
            pltpu.VMEM((4, 4, 24, LANES), F32),
            pltpu.VMEM((4, 4, 24, LANES), F32),
            dma(24), dma(18), dma(8), dma(4),
        ],
        compiler_params=pltpu.CompilerParams(vmem_limit_bytes=VMEM_BYTES),
        name="first",
    )(info, *arrays)


def second(info, *arrays):
    return pl.pallas_call(
        second_kernel,
        out_shape=[PIECE] * 8,
        in_specs=[SMEM] + [ANY] * 30,
        out_specs=[ANY] * 8,
        scratch_shapes=[
            pltpu.VMEM((TERMS, 6, ROWS, LANES), F32),
            pltpu.VMEM((TERMS, 4, ROWS, LANES), F32),
            pltpu.VMEM((TERMS, ROWS, LANES), F32),
            pltpu.VMEM((TERMS, 4, ROWS, LANES), F32),
            pltpu.VMEM((DIM + 1, 4, ROWS, LANES), F32),
            pltpu.VMEM((4, 4, 24, LANES), F32),
            pltpu.VMEM((4, 4, 24, LANES), F32),
            dma(24), dma(6), dma(8),
        ],
        compiler_params=pltpu.CompilerParams(vmem_limit_bytes=VMEM_BYTES),
        name="second",
    )(info, *arrays)


BAND = ("half", "term")
ORDER = (4, 6, 2, 5, 7, 3, 1)


def exchange(pieces):
    got = [None] * 8
    got[0] = pieces[0]
    for k in ORDER:
        got[k] = lax.ppermute(pieces[k], BAND, [(i, i ^ k) for i in range(8)])
    return got


def unpacked(got, band):
    whole = jnp.zeros((T4, 2, 128, LANES), F32)
    for k in range(8):
        start = jnp.bitwise_xor(band, k) * ROWS
        whole = lax.dynamic_update_slice(whole, got[k], (0, 0, start, 0))
    return whole


def shards(right_side, mean_cond, cond_terms):
    quads = lax.axis_size("quad")
    band = lax.axis_index(BAND)
    h, t = band // 4, band % 4
    info = jnp.stack([h, t, band % 2]).astype(jnp.int32)

    outer = exchange(pack(jnp.stack([h, band]).astype(jnp.int32), right_side))
    inner = exchange(pack(jnp.stack([1 - h, band]).astype(jnp.int32), right_side))

    local = jnp.concatenate([mean_cond[None], cond_terms], axis=0)
    own = lax.dynamic_slice_in_dim(local, h * ROWS, ROWS, axis=2)
    rest = lax.dynamic_slice_in_dim(local, (1 - h) * ROWS, ROWS, axis=2)
    near = lax.ppermute(own, BAND, [(4 * a + b, 2 * b + a) for a in range(2) for b in range(4)])
    far = lax.ppermute(rest, BAND, [(4 * a + b, 2 * b + 1 - a) for a in range(2) for b in range(4)])

    def z_shift(arrays, lower_half):
        face = jnp.concatenate([a[:T4] for a in arrays], axis=0)
        pairs = []
        for q in range(quads):
            for b in range(8):
                other = q - 1 if (b // 4) == lower_half else q + 1
                if 0 <= other < quads:
                    pairs.append((q * 8 + b, other * 8 + b))
        return lax.ppermute(face, ("quad", "half", "term"), pairs)

    zlo = z_shift(outer[0:4], 0)
    zhi = z_shift(outer[4:8], 1)

    made = first(info, *outer, *inner, zlo, zhi, near, far)
    sol, (z0, z3, y0, y15) = made[:8], made[8:]

    up = [(i, i + 1) for i in range(quads - 1)]
    down = [(i + 1, i) for i in range(quads - 1)]
    below = lax.ppermute(z3, "quad", up)
    above = lax.ppermute(z0, "quad", down)
    yup = lax.ppermute(y15, BAND, [(i, i + 1) for i in range(7)])
    ydn = lax.ppermute(y0, BAND, [(i + 1, i) for i in range(7)])

    solution = unpacked(exchange(sol), band)
    res = second(info, *outer, *inner, *sol, below, above, yup, ydn, near, far)
    residual = unpacked(exchange(res), band)
    return (solution, residual)


def solution(mesh):
    grid = Mesh(mesh.devices.reshape(-1, 2, 4), ("quad", "half", "term"))
    field = P("term", ("quad", "half"), None, None)
    return jax.shard_map(
        shards,
        mesh=grid,
        in_specs=(field, P(("quad", "half"), "term", None), P(None, ("quad", "half"), "term", None)),
        out_specs=(field, field),
        check_vma=False,
    )
```

```python
import functools
import math

import jax
import jax.numpy as jnp
from jax import lax
from jax.experimental import pallas as pl
from jax.experimental.pallas import tpu as pltpu
from jax.sharding import Mesh, PartitionSpec as P

DIM = 6
DEG = 3
LOWER = 2.0
UPPER = 72.0

TERMS = 84
T4 = 21
ROWS = 16
LANES = 128
F32 = jnp.float32
WEIGHT = pl.CostEstimate(flops=10**12, transcendentals=0, bytes_accessed=10**9)
VMEM_BYTES = 20 * 1024 * 1024


def compositions(degree_sum, slots_left):
    if slots_left == 1:
        return [[degree_sum]]
    listing = []
    for leading in range(degree_sum, -1, -1):
        for remainder in compositions(degree_sum - leading, slots_left - 1):
            listing.append([leading] + remainder)
    return listing


def couplings(variables, degree):
    indices = []
    for level in range(degree + 1):
        indices.extend(compositions(level, variables))
    place = {tuple(m): n for n, m in enumerate(indices)}
    result = []
    for first in indices:
        found = []
        for k in range(variables):
            for step in (-1, 1):
                other = list(first)
                other[k] += step
                j = place.get(tuple(other))
                if j is not None:
                    found.append((j, k, max(first[k], other[k])))
        result.append(found)
    return result


def scalars():
    center = 0.5 * (UPPER + LOWER)
    half = 0.5 * (UPPER - LOWER)
    sigma = center / half
    rho0 = 1.0 / sigma
    rho1 = 1.0 / (2.0 * sigma - rho0)
    keep = (1.0 + rho1 * rho0) / center + 2.0 * rho1 / half
    mix = -2.0 * rho1 / half / center
    return keep, mix


COUPLE = couplings(DIM, DEG)
MEANS = [n / math.sqrt(4.0 * n * n - 1.0) for n in range(1, DEG + 1)]
KEEP, MIX = scalars()

HBM = pl.BlockSpec(memory_space=pltpu.HBM)
SMEM = pl.BlockSpec(memory_space=pltpu.SMEM)
BANDS = 8


def held(*shape):
    return pltpu.HBM(shape, F32)


def fixed(array):
    return pltpu.with_memory_space_constraint(array, pltpu.HBM)


def dma(count):
    return pltpu.SemaphoreType.DMA((count,))


def pack_kernel(split, s_ref, x_ref, *refs):
    count = BANDS if split else 1
    outs, (xv, hv, sem_in, sem_main, sem_halo) = refs[:count], refs[count:]
    h = s_ref[0]
    band = 4 * h + s_ref[1]
    load = pltpu.make_async_copy(x_ref.at[:, h if split else 1 - h], xv, sem_in)
    load.start()
    load.wait()
    copies = []
    for k in range(BANDS):
        if split:
            d, out = jnp.bitwise_xor(band, k), outs[k]
            rows = pl.ds(pl.multiple_of(d * ROWS, ROWS), ROWS)
            above = jnp.maximum(d * ROWS - 1, 0)
            below = jnp.minimum(d * ROWS + ROWS, 127)
        else:
            d, out = k, outs[0].at[k]
            rows = pl.ds(d * ROWS, ROWS)
            above, below = max(d * ROWS - 1, 0), min(d * ROWS + ROWS, 127)
        c = pltpu.make_async_copy(xv.at[:, rows, :], out.at[pl.ds(0, T4)], sem_main.at[k])
        c.start()
        copies.append(c)
        for j in range(T4):
            up = xv[j, pl.ds(above, 1), :]
            dn = xv[j, pl.ds(below, 1), :]
            up = jnp.where(d == 0, jnp.zeros_like(up), up)
            dn = jnp.where(d == BANDS - 1, jnp.zeros_like(dn), dn)
            a, b = j, 24 + j
            hv[k, a // 16, pl.ds(a % 16, 1), :] = up
            hv[k, b // 16, pl.ds(b % 16, 1), :] = dn
        c = pltpu.make_async_copy(hv.at[k], out.at[pl.ds(T4, 3)], sem_halo.at[k])
        c.start()
        copies.append(c)
    for c in copies:
        c.wait()


def pack(split, info, x):
    return pl.pallas_call(
        functools.partial(pack_kernel, split),
        out_shape=[held(24, ROWS, LANES)] * BANDS if split else [held(BANDS, 24, ROWS, LANES)],
        in_specs=[SMEM, HBM],
        out_specs=[HBM] * (BANDS if split else 1),
        scratch_shapes=[
            pltpu.VMEM((T4, 128, LANES), F32),
            pltpu.VMEM((BANDS, 3, ROWS, LANES), F32),
            pltpu.SemaphoreType.DMA, dma(8), dma(8),
        ],
        compiler_params=pltpu.CompilerParams(vmem_limit_bytes=VMEM_BYTES),
        name="pack_edge" if split else "pack_middle",
    )(info, fixed(x))


def start_all(pairs, sems):
    copies = [pltpu.make_async_copy(a, b, sems.at[n]) for n, (a, b) in enumerate(pairs)]
    for c in copies:
        c.start()
    return copies


def weigh(cond, w, planes, scale):
    for p in planes:
        w[p, 0] = scale * cond[0, p]
        for k in range(DIM):
            for n in range(DEG):
                w[p, 1 + DEG * k + n] = (scale * MEANS[n]) * cond[k + 1, p]


def laplace_plane(v, lap, p, zero, up_row, dn_row):
    lane = lax.broadcasted_iota(jnp.int32, (ROWS, LANES), 1)
    first_lane, last_lane = lane == 0, lane == LANES - 1
    rows = pl.ds(TOP, ROWS)

    def group(t, carry):
        for jj in range(T4):
            j = t * T4 + jj
            v[j, p + 1, pl.ds(TOP - 1, 1), :] = up_row(t, p, jj)
            v[j, p + 1, pl.ds(TOP + ROWS, 1), :] = dn_row(t, p, jj)
        for jj in range(T4):
            j = t * T4 + jj
            c = v[j, p + 1, rows, :]
            up = v[j, p + 1, pl.ds(zero + (TOP - 1), ROWS), :]
            dn = v[j, p + 1, pl.ds(zero + (TOP + 1), ROWS), :]
            right = jnp.where(last_lane, 0.0, pltpu.roll(c, LANES - 1, 1))
            left = jnp.where(first_lane, 0.0, pltpu.roll(c, 1, 1))
            beside = v[j, p + 2, rows, :] + v[j, p, rows, :]
            beside = beside + dn + up
            beside = beside + right + left
            lap[j] = 6.0 * c - beside
        return carry

    lax.fori_loop(0, 4, group, 0)


def couple_plane(lap, w, p, emit):
    for half in range(2):
        rows = pl.ds(8 * half, 8)
        weights = [w[p, m, rows, :] for m in range(1 + DEG * DIM)]
        for i in range(TERMS):
            acc = weights[0] * lap[i, rows, :]
            for j, k, n in COUPLE[i]:
                acc = acc + weights[DEG * k + n] * lap[j, rows, :]
            emit(i, half, acc)


def waiting(groups, sems):
    at, held_back = 0, []
    for pairs in groups:
        copies = []
        for a, b in pairs:
            copies.append(pltpu.make_async_copy(a, b, sems.at[at]))
            at += 1
        for c in copies:
            c.start()
        held_back.append(copies)
    return held_back


def place_of(s_ref, k):
    h = jnp.bitwise_xor(s_ref[0], k >> 2)
    t = jnp.bitwise_xor(s_ref[1], k & 3)
    return h, t


def conductivity_pairs(s_ref, near, far, cond):
    odd = s_ref[2]
    return [
        (near, cond.at[:, pl.ds(2 * odd, 2)]),
        (far, cond.at[:, pl.ds(2 * (1 - odd), 2)]),
    ]


def first_kernel(edge, s_ref, *refs):
    outer, inner, near, far = refs[0:8], refs[8], refs[9], refs[10]
    if edge:
        zlo, zhi = refs[11:13]
        sol, y0, y15, z0, z3 = refs[15:20]
        scratch = refs[20:]
    else:
        sol, y0, y15 = refs[11:14]
        scratch = refs[14:]
    v, halo, lap, out, cond, w, y0v, y15v, sem_v, sem_o, sem_e = scratch
    h, zero = s_ref[0], s_ref[3]
    planes = (0, 3) if edge else (1, 2)
    rows = pl.ds(TOP, ROWS)

    early = conductivity_pairs(s_ref, near, far, cond)
    late = []
    for n in range(8):
        hk, tk = n // 4, n % 4
        group = late if edge and hk == 1 else early
        group.append((inner.at[n, pl.ds(0, T4)], v.at[pl.ds(tk * T4, T4), 2 + hk, rows]))
        if not edge:
            early.append((inner.at[n, pl.ds(T4, 3)], halo.at[tk, 1 + hk]))
        hk, tk = place_of(s_ref, n)
        early.append((outer[n].at[pl.ds(0, T4)], v.at[pl.ds(tk * T4, T4), 3 * hk + 1, rows]))
        if edge:
            early.append((outer[n].at[pl.ds(T4, 3)], halo.at[tk, 3 * hk]))
    if edge:
        for k in range(4):
            _, tk = place_of(s_ref, k)
            terms = pl.ds(tk * T4, T4)
            early.append((zlo.at[pl.ds(k * T4, T4)], v.at[terms, 5 * (1 - h), rows]))
            early.append((zhi.at[pl.ds(k * T4, T4)], v.at[terms, 5 * h, rows]))
    early, late = waiting([early, late], sem_v)
    for t in range(4):
        for n in planes:
            y0v[t, n, T4:24, :] = jnp.zeros((24 - T4, LANES), F32)
            y15v[t, n, T4:24, :] = jnp.zeros((24 - T4, LANES), F32)
    for c in early:
        c.wait()
    weigh(cond, w, planes, MIX)

    def up_row(t, p, jj):
        return halo[t, p, jj // 16, pl.ds(jj % 16, 1), :]

    def dn_row(t, p, jj):
        return halo[t, p, (24 + jj) // 16, pl.ds((24 + jj) % 16, 1), :]

    def plane_step(n, carry):
        @pl.when(n == 1)
        def _():
            for c in late:
                c.wait()

        p = planes[0] + (planes[1] - planes[0]) * n
        laplace_plane(v, lap, p, zero, up_row, dn_row)

        def emit(i, half, acc):
            value = KEEP * v[i, p + 1, pl.ds(TOP + 8 * half, 8), :] + acc
            out[i, p, pl.ds(8 * half, 8), :] = value
            if half == 0:
                y0v[i // T4, p, pl.ds(i % T4, 1), :] = value[0:1]
            else:
                y15v[i // T4, p, pl.ds(i % T4, 1), :] = value[7:8]

        couple_plane(lap, w, p, emit)
        for c in sends(out, sol, sem_o, p):
            c.start()
        if edge:
            for m in range(2):

                @pl.when(n == m)
                def _():
                    face(m).start()

        return carry

    def face(m):
        return pltpu.make_async_copy(out.at[:, planes[m]], (z0, z3)[m], sem_e.at[4 + m])

    lax.fori_loop(0, 2, plane_step, 0)
    ends = [(a.at[:, p], b.at[:, p]) for p in planes for a, b in ((y0v, y0), (y15v, y15))]
    ends = start_all(ends, sem_e)
    if edge:
        ends += [face(0), face(1)]
    for c in ends:
        c.wait()
    for p in planes:
        for c in sends(out, sol, sem_o, p):
            c.wait()


def sends(out, to, sem, p):
    half = p // 2
    return [
        pltpu.make_async_copy(
            out.at[pl.ds(t * T4, T4), p], to.at[half * 4 + t], sem.at[p * 4 + t]
        )
        for t in range(4)
    ]


def second_kernel(s_ref, *refs):
    outer, (inner, middle, edge, below, above, yup, ydn, near, far) = refs[0:8], refs[8:17]
    outs = refs[17:25]
    v, r, lap, out, cond, w, upv, dnv, sem_v, sem_o = refs[25:]
    h, zero = s_ref[0], s_ref[3]
    rows = pl.ds(TOP, ROWS)

    groups = [[(yup, upv), (ydn, dnv), (below, v.at[:, 0, rows])], [], [], []]
    groups[0] += conductivity_pairs(s_ref, near, far, cond)
    for n in range(8):
        hk, tk = n // 4, n % 4
        terms = pl.ds(tk * T4, T4)
        groups[hk].append((middle.at[n], v.at[terms, 2 + hk, rows]))
        groups[2 * hk].append((edge.at[n], v.at[terms, 1 + 3 * hk, rows]))
        groups[hk].append((inner.at[n, pl.ds(0, T4)], r.at[terms, 1 + hk]))
        hk, tk = place_of(s_ref, n)
        groups[0].append((outer[n].at[pl.ds(0, T4)], r.at[pl.ds(tk * T4, T4), 3 * hk]))
    groups[3].append((above, v.at[:, 5, rows]))
    groups = waiting(groups, sem_v)
    for c in groups[0]:
        c.wait()
    weigh(cond, w, range(4), -1.0)

    def up_row(t, p, jj):
        return upv[t, p, pl.ds(jj, 1), :]

    def dn_row(t, p, jj):
        return dnv[t, p, pl.ds(jj, 1), :]

    def scattered(group):
        result = []
        for kk in range(4):
            k = group * 4 + kk
            hk, tk = place_of(s_ref, k)
            result.append(
                pltpu.make_async_copy(
                    out.at[pl.ds(tk * T4, T4), pl.ds(2 * hk, 2)], outs[k], sem_o.at[k]
                )
            )
        return result

    def plane_step(p, carry):
        for m in range(1, 4):

            @pl.when(p == m)
            def _():
                for c in groups[m]:
                    c.wait()

        laplace_plane(v, lap, p, zero, up_row, dn_row)

        def emit(i, half, acc):
            own = pl.ds(8 * half, 8)
            out[i, p, own, :] = r[i, p, own, :] + acc

        couple_plane(lap, w, p, emit)
        for group in range(2):

            @pl.when((p % 2 == 1) & (jnp.bitwise_xor(h, group) == p // 2))
            def _():
                for c in scattered(group):
                    c.start()

        return carry

    lax.fori_loop(0, 4, plane_step, 0)
    for c in scattered(0) + scattered(1):
        c.wait()


TOP = 8
PIECE = held(T4, 2, ROWS, LANES)
PIECES = held(BANDS, T4, ROWS, LANES)
FACE = held(TERMS, ROWS, LANES)
EDGE = held(4, 4, 24, LANES)
RES_SHAPES = [PIECE] * 8


def first(edge, info, *arrays):
    return pl.pallas_call(
        functools.partial(first_kernel, edge),
        out_shape=[PIECES, EDGE, EDGE] + ([FACE, FACE] if edge else []),
        in_specs=[SMEM] + [HBM] * len(arrays),
        out_specs=[HBM] * (5 if edge else 3),
        scratch_shapes=[
            pltpu.VMEM((TERMS, 6, 32, LANES), F32),
            pltpu.VMEM((4, 4, 3, ROWS, LANES), F32),
            pltpu.VMEM((TERMS, ROWS, LANES), F32),
            pltpu.VMEM((TERMS, 4, ROWS, LANES), F32),
            pltpu.VMEM((DIM + 1, 4, ROWS, LANES), F32),
            pltpu.VMEM((4, 1 + DEG * DIM, ROWS, LANES), F32),
            pltpu.VMEM((4, 4, 24, LANES), F32),
            pltpu.VMEM((4, 4, 24, LANES), F32),
            dma(34), dma(16), dma(6),
        ],
        compiler_params=pltpu.CompilerParams(vmem_limit_bytes=VMEM_BYTES),
        input_output_aliases={14: 1, 15: 2} if edge else {},
        name="first_edge" if edge else "first_middle",
    )(info, *arrays)


def second(info, *arrays):
    return pl.pallas_call(
        second_kernel,
        out_shape=RES_SHAPES,
        in_specs=[SMEM] + [HBM] * 17,
        out_specs=[HBM] * len(RES_SHAPES),
        scratch_shapes=[
            pltpu.VMEM((TERMS, 6, 32, LANES), F32),
            pltpu.VMEM((TERMS, 4, ROWS, LANES), F32),
            pltpu.VMEM((TERMS, ROWS, LANES), F32),
            pltpu.VMEM((TERMS, 4, ROWS, LANES), F32),
            pltpu.VMEM((DIM + 1, 4, ROWS, LANES), F32),
            pltpu.VMEM((4, 1 + DEG * DIM, ROWS, LANES), F32),
            pltpu.VMEM((4, 4, 24, LANES), F32),
            pltpu.VMEM((4, 4, 24, LANES), F32),
            dma(38), dma(8),
        ],
        compiler_params=pltpu.CompilerParams(vmem_limit_bytes=VMEM_BYTES),
        cost_estimate=WEIGHT,
        name="second",
    )(info, *arrays)


BAND = ("half", "term")
ORDER = (4, 2, 6, 5, 3, 7, 1)


def swapped(pieces):
    return lax.all_to_all(pieces, BAND, 0, 0, tiled=True)


def exchange(pieces):
    got = [None] * 8
    got[0] = pieces[0]
    for k in ORDER:
        got[k] = lax.ppermute(pieces[k], BAND, [(i, i ^ k) for i in range(8)])
    return got


def unpacked(got, band, other):
    whole = jnp.zeros((T4, 2, 128, LANES), F32)
    for n, k in enumerate((0,) + ORDER):
        if n == 5:
            whole, other = lax.optimization_barrier((whole, other))
        start = jnp.bitwise_xor(band, k) * ROWS
        whole = lax.dynamic_update_slice(whole, got[k], (0, 0, start, 0))
    return whole, other


def joined(pieces):
    return jnp.transpose(pieces, (1, 0, 2, 3)).reshape(T4, 128, LANES)


def shards(right_side, mean_cond, cond_terms):
    quads = lax.axis_size("quad")
    band = lax.axis_index(BAND)
    h, t = band // 4, band % 4
    info = jnp.stack([h, t, band % 2, 0 * band]).astype(jnp.int32)
    up = [(i, i + 1) for i in range(quads - 1)]
    down = [(i + 1, i) for i in range(quads - 1)]

    outer = exchange(pack(True, info, right_side))
    inner = pack(False, info, right_side)[0]
    inner, *outer[2:] = lax.optimization_barrier((inner, *outer[2:]))
    inner = swapped(inner)

    def z_shift(arrays, lower_half):
        face = jnp.concatenate([a[:T4] for a in arrays], axis=0)
        pairs = []
        for q in range(quads):
            for b in range(BANDS):
                other = q - 1 if (b // 4) == lower_half else q + 1
                if 0 <= other < quads:
                    pairs.append((q * BANDS + b, other * BANDS + b))
        return lax.ppermute(face, ("quad",) + BAND, pairs)

    zlo = z_shift(outer[0:4], 0)
    zhi = z_shift(outer[4:8], 1)

    local = jnp.concatenate([mean_cond[None], cond_terms], axis=0)
    own = lax.dynamic_slice_in_dim(local, h * ROWS, ROWS, axis=2)
    rest = lax.dynamic_slice_in_dim(local, (1 - h) * ROWS, ROWS, axis=2)
    near = lax.ppermute(own, BAND, [(4 * a + b, 2 * b + a) for a in range(2) for b in range(4)])
    far = lax.ppermute(rest, BAND, [(4 * a + b, 2 * b + 1 - a) for a in range(2) for b in range(4)])

    sol_middle, y0, y15 = first(False, info, *outer, inner, near, far)
    sol_edge, y0, y15, z0, z3 = first(True, info, *outer, inner, near, far, zlo, zhi, y0, y15)

    below = lax.ppermute(z3, "quad", up)
    above = lax.ppermute(z0, "quad", down)
    yup = lax.ppermute(y15, BAND, [(i, i + 1) for i in range(7)])
    ydn = lax.ppermute(y0, BAND, [(i + 1, i) for i in range(7)])

    solution = jnp.zeros((T4, 2, 128, LANES), F32)
    for plane, part in ((1 - h, swapped(sol_middle)), (h, swapped(sol_edge))):
        solution = lax.dynamic_update_slice(solution, joined(part)[:, None], (0, plane, 0, 0))
    res = second(
        info, *outer, inner, fixed(sol_middle), fixed(sol_edge), below, above, yup, ydn, near, far
    )
    residual, solution = unpacked(exchange(res), band, solution)
    return (solution, residual)


def solution(mesh):
    grid = Mesh(mesh.devices.reshape(-1, 2, 4), ("quad", "half", "term"))
    field = P("term", ("quad", "half"), None, None)
    return jax.shard_map(
        shards,
        mesh=grid,
        in_specs=(field, P(("quad", "half"), "term", None), P(None, ("quad", "half"), "term", None)),
        out_specs=(field, field),
        check_vma=False,
    )
```

```python
import functools
import math

import jax
import jax.numpy as jnp
from jax import lax
from jax.experimental import pallas as pl
from jax.experimental.pallas import tpu as pltpu
from jax.sharding import Mesh, PartitionSpec as P

DIM = 6
DEG = 3
LOWER = 2.0
UPPER = 72.0

TERMS = 84
T4 = 21
ROWS = 16
LANES = 128
F32 = jnp.float32
WEIGHT = pl.CostEstimate(flops=10**12, transcendentals=0, bytes_accessed=10**9)
VMEM_BYTES = 20 * 1024 * 1024


def compositions(degree_sum, slots_left):
    if slots_left == 1:
        return [[degree_sum]]
    listing = []
    for leading in range(degree_sum, -1, -1):
        for remainder in compositions(degree_sum - leading, slots_left - 1):
            listing.append([leading] + remainder)
    return listing


def couplings(variables, degree):
    indices = []
    for level in range(degree + 1):
        indices.extend(compositions(level, variables))
    place = {tuple(m): n for n, m in enumerate(indices)}
    result = []
    for first in indices:
        found = []
        for k in range(variables):
            for step in (-1, 1):
                other = list(first)
                other[k] += step
                j = place.get(tuple(other))
                if j is not None:
                    found.append((j, k, max(first[k], other[k])))
        result.append(found)
    return result


def scalars():
    center = 0.5 * (UPPER + LOWER)
    half = 0.5 * (UPPER - LOWER)
    sigma = center / half
    rho0 = 1.0 / sigma
    rho1 = 1.0 / (2.0 * sigma - rho0)
    keep = (1.0 + rho1 * rho0) / center + 2.0 * rho1 / half
    mix = -2.0 * rho1 / half / center
    return keep, mix


COUPLE = couplings(DIM, DEG)
MEANS = [n / math.sqrt(4.0 * n * n - 1.0) for n in range(1, DEG + 1)]
KEEP, MIX = scalars()

HBM = pl.BlockSpec(memory_space=pltpu.HBM)
SMEM = pl.BlockSpec(memory_space=pltpu.SMEM)
BANDS = 8


def held(*shape):
    return pltpu.HBM(shape, F32)


def fixed(array):
    return pltpu.with_memory_space_constraint(array, pltpu.HBM)


def dma(count):
    return pltpu.SemaphoreType.DMA((count,))


def pack_kernel(split, s_ref, x_ref, *refs):
    count = BANDS if split else 1
    outs, (xv, hv, sem_in, sem_main, sem_halo) = refs[:count], refs[count:]
    h = s_ref[0]
    band = 4 * h + s_ref[1]
    load = pltpu.make_async_copy(x_ref.at[:, h if split else 1 - h], xv, sem_in)
    load.start()
    load.wait()
    copies = []
    for k in range(BANDS):
        if split:
            d, out = jnp.bitwise_xor(band, k), outs[k]
            rows = pl.ds(pl.multiple_of(d * ROWS, ROWS), ROWS)
            above = jnp.maximum(d * ROWS - 1, 0)
            below = jnp.minimum(d * ROWS + ROWS, 127)
        else:
            d, out = k, outs[0].at[k]
            rows = pl.ds(d * ROWS, ROWS)
            above, below = max(d * ROWS - 1, 0), min(d * ROWS + ROWS, 127)
        c = pltpu.make_async_copy(xv.at[:, rows, :], out.at[pl.ds(0, T4)], sem_main.at[k])
        c.start()
        copies.append(c)
        for j in range(T4):
            up = xv[j, pl.ds(above, 1), :]
            dn = xv[j, pl.ds(below, 1), :]
            up = jnp.where(d == 0, jnp.zeros_like(up), up)
            dn = jnp.where(d == BANDS - 1, jnp.zeros_like(dn), dn)
            a, b = j, 24 + j
            hv[k, a // 16, pl.ds(a % 16, 1), :] = up
            hv[k, b // 16, pl.ds(b % 16, 1), :] = dn
        c = pltpu.make_async_copy(hv.at[k], out.at[pl.ds(T4, 3)], sem_halo.at[k])
        c.start()
        copies.append(c)
    for c in copies:
        c.wait()


def pack(split, info, x):
    return pl.pallas_call(
        functools.partial(pack_kernel, split),
        out_shape=[held(24, ROWS, LANES)] * BANDS if split else [held(BANDS, 24, ROWS, LANES)],
        in_specs=[SMEM, HBM],
        out_specs=[HBM] * (BANDS if split else 1),
        scratch_shapes=[
            pltpu.VMEM((T4, 128, LANES), F32),
            pltpu.VMEM((BANDS, 3, ROWS, LANES), F32),
            pltpu.SemaphoreType.DMA, dma(8), dma(8),
        ],
        compiler_params=pltpu.CompilerParams(vmem_limit_bytes=VMEM_BYTES),
        name="pack_edge" if split else "pack_middle",
    )(info, fixed(x))


def faces_kernel(*refs):
    pieces, faces, (held_v, sems) = refs[:BANDS], refs[BANDS : BANDS + 2], refs[BANDS + 2 :]
    loads = start_all(
        [
            (pieces[k].at[pl.ds(0, T4)], held_v.at[k // 4, pl.ds(k % 4 * T4, T4)])
            for k in range(BANDS)
        ],
        sems,
    )
    for c in loads:
        c.wait()
    stores = start_all([(held_v.at[n], faces[n]) for n in range(2)], sems)
    for c in stores:
        c.wait()


def faces(*pieces):
    return pl.pallas_call(
        faces_kernel,
        out_shape=[held(TERMS, ROWS, LANES)] * 2,
        in_specs=[HBM] * BANDS,
        out_specs=[HBM] * 2,
        scratch_shapes=[pltpu.VMEM((2, TERMS, ROWS, LANES), F32), dma(BANDS)],
        compiler_params=pltpu.CompilerParams(vmem_limit_bytes=VMEM_BYTES),
        cost_estimate=WEIGHT,
        name="faces",
    )(*pieces)


def start_all(pairs, sems):
    copies = [pltpu.make_async_copy(a, b, sems.at[n]) for n, (a, b) in enumerate(pairs)]
    for c in copies:
        c.start()
    return copies


def weigh(cond, w, planes, scale):
    for p in planes:
        w[p, 0] = scale * cond[0, p]
        for k in range(DIM):
            for n in range(DEG):
                w[p, 1 + DEG * k + n] = (scale * MEANS[n]) * cond[k + 1, p]


def laplace_plane(v, lap, p, zero, up_row, dn_row):
    lane = lax.broadcasted_iota(jnp.int32, (ROWS, LANES), 1)
    first_lane, last_lane = lane == 0, lane == LANES - 1
    rows = pl.ds(TOP, ROWS)

    def group(t, carry):
        for jj in range(T4):
            j = t * T4 + jj
            v[j, p + 1, pl.ds(TOP - 1, 1), :] = up_row(t, p, jj)
            v[j, p + 1, pl.ds(TOP + ROWS, 1), :] = dn_row(t, p, jj)
        for jj in range(T4):
            j = t * T4 + jj
            c = v[j, p + 1, rows, :]
            up = v[j, p + 1, pl.ds(zero + (TOP - 1), ROWS), :]
            dn = v[j, p + 1, pl.ds(zero + (TOP + 1), ROWS), :]
            right = jnp.where(last_lane, 0.0, pltpu.roll(c, LANES - 1, 1))
            left = jnp.where(first_lane, 0.0, pltpu.roll(c, 1, 1))
            beside = v[j, p + 2, rows, :] + v[j, p, rows, :]
            beside = beside + dn + up
            beside = beside + right + left
            lap[j] = 6.0 * c - beside
        return carry

    lax.fori_loop(0, 4, group, 0)


def couple_plane(lap, w, p, emit):
    for half in range(2):
        rows = pl.ds(8 * half, 8)
        weights = [w[p, m, rows, :] for m in range(1 + DEG * DIM)]
        for i in range(TERMS):
            acc = weights[0] * lap[i, rows, :]
            for j, k, n in COUPLE[i]:
                acc = acc + weights[DEG * k + n] * lap[j, rows, :]
            emit(i, half, acc)


def waiting(groups, sems):
    at, held_back = 0, []
    for pairs in groups:
        copies = []
        for a, b in pairs:
            copies.append(pltpu.make_async_copy(a, b, sems.at[at]))
            at += 1
        for c in copies:
            c.start()
        held_back.append(copies)
    return held_back


def place_of(s_ref, k):
    h = jnp.bitwise_xor(s_ref[0], k >> 2)
    t = jnp.bitwise_xor(s_ref[1], k & 3)
    return h, t


def conductivity_pairs(s_ref, near, far, cond):
    odd = s_ref[2]
    return [
        (near, cond.at[:, pl.ds(2 * odd, 2)]),
        (far, cond.at[:, pl.ds(2 * (1 - odd), 2)]),
    ]


def first_kernel(edge, s_ref, *refs):
    outer, inner, near, far = refs[0:8], refs[8], refs[9], refs[10]
    if edge:
        zlo, zhi = refs[11:13]
        sol, y0, y15, z0, z3 = refs[15:20]
        scratch = refs[20:]
    else:
        sol, y0, y15 = refs[11:14]
        scratch = refs[14:]
    v, halo, lap, out, cond, w, y0v, y15v, sem_v, sem_o, sem_e = scratch
    h, zero = s_ref[0], s_ref[3]
    planes = (0, 3) if edge else (1, 2)
    rows = pl.ds(TOP, ROWS)

    early = conductivity_pairs(s_ref, near, far, cond)
    late = []
    for n in range(8):
        hk, tk = n // 4, n % 4
        group = late if edge and hk == 1 else early
        group.append((inner.at[n, pl.ds(0, T4)], v.at[pl.ds(tk * T4, T4), 2 + hk, rows]))
        if not edge:
            early.append((inner.at[n, pl.ds(T4, 3)], halo.at[tk, 1 + hk]))
        hk, tk = place_of(s_ref, n)
        early.append((outer[n].at[pl.ds(0, T4)], v.at[pl.ds(tk * T4, T4), 3 * hk + 1, rows]))
        if edge:
            early.append((outer[n].at[pl.ds(T4, 3)], halo.at[tk, 3 * hk]))
    if edge:
        for k in range(4):
            _, tk = place_of(s_ref, k)
            terms = pl.ds(tk * T4, T4)
            early.append((zlo.at[pl.ds(k * T4, T4)], v.at[terms, 5 * (1 - h), rows]))
            early.append((zhi.at[pl.ds(k * T4, T4)], v.at[terms, 5 * h, rows]))
    early, late = waiting([early, late], sem_v)
    for t in range(4):
        for n in planes:
            y0v[t, n, T4:24, :] = jnp.zeros((24 - T4, LANES), F32)
            y15v[t, n, T4:24, :] = jnp.zeros((24 - T4, LANES), F32)
    for c in early:
        c.wait()
    weigh(cond, w, planes, MIX)

    def up_row(t, p, jj):
        return halo[t, p, jj // 16, pl.ds(jj % 16, 1), :]

    def dn_row(t, p, jj):
        return halo[t, p, (24 + jj) // 16, pl.ds((24 + jj) % 16, 1), :]

    def plane_step(n, carry):
        @pl.when(n == 1)
        def _():
            for c in late:
                c.wait()

        p = planes[0] + (planes[1] - planes[0]) * n
        laplace_plane(v, lap, p, zero, up_row, dn_row)

        def emit(i, half, acc):
            value = KEEP * v[i, p + 1, pl.ds(TOP + 8 * half, 8), :] + acc
            out[i, p, pl.ds(8 * half, 8), :] = value
            if half == 0:
                y0v[i // T4, p, pl.ds(i % T4, 1), :] = value[0:1]
            else:
                y15v[i // T4, p, pl.ds(i % T4, 1), :] = value[7:8]

        couple_plane(lap, w, p, emit)
        for c in sends(out, sol, sem_o, p):
            c.start()
        if edge:
            for m in range(2):

                @pl.when(n == m)
                def _():
                    face(m).start()

        return carry

    def face(m):
        return pltpu.make_async_copy(out.at[:, planes[m]], (z0, z3)[m], sem_e.at[4 + m])

    lax.fori_loop(0, 2, plane_step, 0)
    ends = [(a.at[:, p], b.at[:, p]) for p in planes for a, b in ((y0v, y0), (y15v, y15))]
    ends = start_all(ends, sem_e)
    if edge:
        ends += [face(0), face(1)]
    for c in ends:
        c.wait()
    for p in planes:
        for c in sends(out, sol, sem_o, p):
            c.wait()


def sends(out, to, sem, p):
    half = p // 2
    return [
        pltpu.make_async_copy(
            out.at[pl.ds(t * T4, T4), p], to.at[half * 4 + t], sem.at[p * 4 + t]
        )
        for t in range(4)
    ]


def second_kernel(s_ref, *refs):
    outer, (inner, middle, edge, below, above, yup, ydn, near, far) = refs[0:8], refs[8:17]
    outs = refs[17:25]
    v, r, lap, out, cond, w, upv, dnv, sem_v, sem_o = refs[25:]
    h, zero = s_ref[0], s_ref[3]
    rows = pl.ds(TOP, ROWS)

    groups = [[(yup, upv), (ydn, dnv), (below, v.at[:, 0, rows])], [], [], []]
    groups[0] += conductivity_pairs(s_ref, near, far, cond)
    for n in range(8):
        hk, tk = n // 4, n % 4
        terms = pl.ds(tk * T4, T4)
        groups[hk].append((middle.at[n], v.at[terms, 2 + hk, rows]))
        groups[2 * hk].append((edge.at[n], v.at[terms, 1 + 3 * hk, rows]))
        groups[hk].append((inner.at[n, pl.ds(0, T4)], r.at[terms, 1 + hk]))
        hk, tk = place_of(s_ref, n)
        groups[0].append((outer[n].at[pl.ds(0, T4)], r.at[pl.ds(tk * T4, T4), 3 * hk]))
    groups[3].append((above, v.at[:, 5, rows]))
    groups = waiting(groups, sem_v)
    for c in groups[0]:
        c.wait()
    weigh(cond, w, range(4), -1.0)

    def up_row(t, p, jj):
        return upv[t, p, pl.ds(jj, 1), :]

    def dn_row(t, p, jj):
        return dnv[t, p, pl.ds(jj, 1), :]

    def scattered(group):
        result = []
        for kk in range(4):
            k = group * 4 + kk
            hk, tk = place_of(s_ref, k)
            result.append(
                pltpu.make_async_copy(
                    out.at[pl.ds(tk * T4, T4), pl.ds(2 * hk, 2)], outs[k], sem_o.at[k]
                )
            )
        return result

    def plane_step(p, carry):
        for m in range(1, 4):

            @pl.when(p == m)
            def _():
                for c in groups[m]:
                    c.wait()

        laplace_plane(v, lap, p, zero, up_row, dn_row)

        def emit(i, half, acc):
            own = pl.ds(8 * half, 8)
            out[i, p, own, :] = r[i, p, own, :] + acc

        couple_plane(lap, w, p, emit)
        for group in range(2):

            @pl.when((p % 2 == 1) & (jnp.bitwise_xor(h, group) == p // 2))
            def _():
                for c in scattered(group):
                    c.start()

        return carry

    lax.fori_loop(0, 4, plane_step, 0)
    for c in scattered(0) + scattered(1):
        c.wait()


TOP = 8
PIECE = held(T4, 2, ROWS, LANES)
PIECES = held(BANDS, T4, ROWS, LANES)
FACE = held(TERMS, ROWS, LANES)
EDGE = held(4, 4, 24, LANES)
RES_SHAPES = [PIECE] * 8


def first(edge, info, *arrays):
    return pl.pallas_call(
        functools.partial(first_kernel, edge),
        out_shape=[PIECES, EDGE, EDGE] + ([FACE, FACE] if edge else []),
        in_specs=[SMEM] + [HBM] * len(arrays),
        out_specs=[HBM] * (5 if edge else 3),
        scratch_shapes=[
            pltpu.VMEM((TERMS, 6, 32, LANES), F32),
            pltpu.VMEM((4, 4, 3, ROWS, LANES), F32),
            pltpu.VMEM((TERMS, ROWS, LANES), F32),
            pltpu.VMEM((TERMS, 4, ROWS, LANES), F32),
            pltpu.VMEM((DIM + 1, 4, ROWS, LANES), F32),
            pltpu.VMEM((4, 1 + DEG * DIM, ROWS, LANES), F32),
            pltpu.VMEM((4, 4, 24, LANES), F32),
            pltpu.VMEM((4, 4, 24, LANES), F32),
            dma(34), dma(16), dma(6),
        ],
        compiler_params=pltpu.CompilerParams(vmem_limit_bytes=VMEM_BYTES),
        input_output_aliases={14: 1, 15: 2} if edge else {},
        name="first_edge" if edge else "first_middle",
    )(info, *arrays)


def second(info, *arrays):
    return pl.pallas_call(
        second_kernel,
        out_shape=RES_SHAPES,
        in_specs=[SMEM] + [HBM] * 17,
        out_specs=[HBM] * len(RES_SHAPES),
        scratch_shapes=[
            pltpu.VMEM((TERMS, 6, 32, LANES), F32),
            pltpu.VMEM((TERMS, 4, ROWS, LANES), F32),
            pltpu.VMEM((TERMS, ROWS, LANES), F32),
            pltpu.VMEM((TERMS, 4, ROWS, LANES), F32),
            pltpu.VMEM((DIM + 1, 4, ROWS, LANES), F32),
            pltpu.VMEM((4, 1 + DEG * DIM, ROWS, LANES), F32),
            pltpu.VMEM((4, 4, 24, LANES), F32),
            pltpu.VMEM((4, 4, 24, LANES), F32),
            dma(38), dma(8),
        ],
        compiler_params=pltpu.CompilerParams(vmem_limit_bytes=VMEM_BYTES),
        cost_estimate=WEIGHT,
        name="second",
    )(info, *arrays)


BAND = ("half", "term")
ORDER = (4, 2, 6, 5, 3, 7, 1)


def swapped(pieces):
    return lax.all_to_all(pieces, BAND, 0, 0, tiled=True)


def exchange(pieces):
    got = [None] * 8
    got[0] = pieces[0]
    for k in ORDER:
        got[k] = lax.ppermute(pieces[k], BAND, [(i, i ^ k) for i in range(8)])
    return got


def unpacked(got, band, other):
    whole = jnp.zeros((T4, 2, 128, LANES), F32)
    for n, k in enumerate((0,) + ORDER):
        if n == 5:
            whole, other = lax.optimization_barrier((whole, other))
        start = jnp.bitwise_xor(band, k) * ROWS
        whole = lax.dynamic_update_slice(whole, got[k], (0, 0, start, 0))
    return whole, other


def joined(pieces):
    return jnp.transpose(pieces, (1, 0, 2, 3)).reshape(T4, 128, LANES)


def shards(right_side, mean_cond, cond_terms):
    quads = lax.axis_size("quad")
    band = lax.axis_index(BAND)
    h, t = band // 4, band % 4
    info = jnp.stack([h, t, band % 2, 0 * band]).astype(jnp.int32)
    up = [(i, i + 1) for i in range(quads - 1)]
    down = [(i + 1, i) for i in range(quads - 1)]

    outer = exchange(pack(True, info, right_side))
    inner = pack(False, info, right_side)[0]
    inner = swapped(inner)

    def z_shift(face, lower_half):
        pairs = []
        for q in range(quads):
            for b in range(BANDS):
                other = q - 1 if (b // 4) == lower_half else q + 1
                if 0 <= other < quads:
                    pairs.append((q * BANDS + b, other * BANDS + b))
        return lax.ppermute(face, ("quad",) + BAND, pairs)

    low, high = faces(*outer)
    zlo = z_shift(low, 0)
    zhi = z_shift(high, 1)

    local = jnp.concatenate([mean_cond[None], cond_terms], axis=0)
    own = lax.dynamic_slice_in_dim(local, h * ROWS, ROWS, axis=2)
    rest = lax.dynamic_slice_in_dim(local, (1 - h) * ROWS, ROWS, axis=2)
    near = lax.ppermute(own, BAND, [(4 * a + b, 2 * b + a) for a in range(2) for b in range(4)])
    far = lax.ppermute(rest, BAND, [(4 * a + b, 2 * b + 1 - a) for a in range(2) for b in range(4)])

    sol_middle, y0, y15 = first(False, info, *outer, inner, near, far)
    sol_edge, y0, y15, z0, z3 = first(True, info, *outer, inner, near, far, zlo, zhi, y0, y15)

    below = lax.ppermute(z3, "quad", up)
    above = lax.ppermute(z0, "quad", down)
    yup = lax.ppermute(y15, BAND, [(i, i + 1) for i in range(7)])
    ydn = lax.ppermute(y0, BAND, [(i + 1, i) for i in range(7)])

    solution = jnp.zeros((T4, 2, 128, LANES), F32)
    for plane, part in ((1 - h, swapped(sol_middle)), (h, swapped(sol_edge))):
        solution = lax.dynamic_update_slice(solution, joined(part)[:, None], (0, plane, 0, 0))
    res = second(
        info, *outer, inner, fixed(sol_middle), fixed(sol_edge), below, above, yup, ydn, near, far
    )
    residual, solution = unpacked(exchange(res), band, solution)
    return (solution, residual)


def solution(mesh):
    grid = Mesh(mesh.devices.reshape(-1, 2, 4), ("quad", "half", "term"))
    field = P("term", ("quad", "half"), None, None)
    return jax.shard_map(
        shards,
        mesh=grid,
        in_specs=(field, P(("quad", "half"), "term", None), P(None, ("quad", "half"), "term", None)),
        out_specs=(field, field),
        check_vma=False,
    )
```

```python
import functools
import math

import jax
import jax.numpy as jnp
from jax import lax
from jax.experimental import pallas as pl
from jax.experimental.pallas import tpu as pltpu
from jax.sharding import Mesh, PartitionSpec as P

DIM = 6
DEG = 3
LOWER = 2.0
UPPER = 72.0

TERMS = 84
T4 = 21
ROWS = 16
LANES = 128
F32 = jnp.float32
WEIGHT = pl.CostEstimate(flops=10**12, transcendentals=0, bytes_accessed=10**9)
VMEM_BYTES = 20 * 1024 * 1024


def compositions(degree_sum, slots_left):
    if slots_left == 1:
        return [[degree_sum]]
    listing = []
    for leading in range(degree_sum, -1, -1):
        for remainder in compositions(degree_sum - leading, slots_left - 1):
            listing.append([leading] + remainder)
    return listing


def couplings(variables, degree):
    indices = []
    for level in range(degree + 1):
        indices.extend(compositions(level, variables))
    place = {tuple(m): n for n, m in enumerate(indices)}
    result = []
    for first in indices:
        found = []
        for k in range(variables):
            for step in (-1, 1):
                other = list(first)
                other[k] += step
                j = place.get(tuple(other))
                if j is not None:
                    found.append((j, k, max(first[k], other[k])))
        result.append(found)
    return result


def scalars():
    center = 0.5 * (UPPER + LOWER)
    half = 0.5 * (UPPER - LOWER)
    sigma = center / half
    rho0 = 1.0 / sigma
    rho1 = 1.0 / (2.0 * sigma - rho0)
    keep = (1.0 + rho1 * rho0) / center + 2.0 * rho1 / half
    mix = -2.0 * rho1 / half / center
    return keep, mix


COUPLE = couplings(DIM, DEG)
MEANS = [n / math.sqrt(4.0 * n * n - 1.0) for n in range(1, DEG + 1)]
KEEP, MIX = scalars()

HBM = pl.BlockSpec(memory_space=pltpu.HBM)
SMEM = pl.BlockSpec(memory_space=pltpu.SMEM)
BANDS = 8


def held(*shape):
    return pltpu.HBM(shape, F32)


def fixed(array):
    return pltpu.with_memory_space_constraint(array, pltpu.HBM)


def dma(count):
    return pltpu.SemaphoreType.DMA((count,))


def pack_kernel(split, s_ref, x_ref, *refs):
    count = BANDS if split else 1
    outs, (xv, hv, sem_in, sem_main, sem_halo) = refs[:count], refs[count:]
    h = s_ref[0]
    band = 4 * h + s_ref[1]
    load = pltpu.make_async_copy(x_ref.at[:, h if split else 1 - h], xv, sem_in)
    load.start()
    load.wait()
    copies = []
    for k in range(BANDS):
        if split:
            d, out = jnp.bitwise_xor(band, k), outs[k]
            rows = pl.ds(pl.multiple_of(d * ROWS, ROWS), ROWS)
            above = jnp.maximum(d * ROWS - 1, 0)
            below = jnp.minimum(d * ROWS + ROWS, 127)
        else:
            d, out = k, outs[0].at[k]
            rows = pl.ds(d * ROWS, ROWS)
            above, below = max(d * ROWS - 1, 0), min(d * ROWS + ROWS, 127)
        c = pltpu.make_async_copy(xv.at[:, rows, :], out.at[pl.ds(0, T4)], sem_main.at[k])
        c.start()
        copies.append(c)
        for j in range(T4):
            up = xv[j, pl.ds(above, 1), :]
            dn = xv[j, pl.ds(below, 1), :]
            up = jnp.where(d == 0, jnp.zeros_like(up), up)
            dn = jnp.where(d == BANDS - 1, jnp.zeros_like(dn), dn)
            a, b = j, 24 + j
            hv[k, a // 16, pl.ds(a % 16, 1), :] = up
            hv[k, b // 16, pl.ds(b % 16, 1), :] = dn
        c = pltpu.make_async_copy(hv.at[k], out.at[pl.ds(T4, 3)], sem_halo.at[k])
        c.start()
        copies.append(c)
    for c in copies:
        c.wait()


def pack(split, info, x):
    return pl.pallas_call(
        functools.partial(pack_kernel, split),
        out_shape=[held(24, ROWS, LANES)] * BANDS if split else [held(BANDS, 24, ROWS, LANES)],
        in_specs=[SMEM, HBM],
        out_specs=[HBM] * (BANDS if split else 1),
        scratch_shapes=[
            pltpu.VMEM((T4, 128, LANES), F32),
            pltpu.VMEM((BANDS, 3, ROWS, LANES), F32),
            pltpu.SemaphoreType.DMA, dma(8), dma(8),
        ],
        compiler_params=pltpu.CompilerParams(vmem_limit_bytes=VMEM_BYTES),
        name="pack_edge" if split else "pack_middle",
    )(info, fixed(x))


def faces_kernel(*refs):
    pieces, faces, (held_v, sems) = refs[:BANDS], refs[BANDS : BANDS + 2], refs[BANDS + 2 :]
    loads = start_all(
        [
            (pieces[k].at[pl.ds(0, T4)], held_v.at[k // 4, pl.ds(k % 4 * T4, T4)])
            for k in range(BANDS)
        ],
        sems,
    )
    for c in loads:
        c.wait()
    stores = start_all([(held_v.at[n], faces[n]) for n in range(2)], sems)
    for c in stores:
        c.wait()


def faces(*pieces):
    return pl.pallas_call(
        faces_kernel,
        out_shape=[held(TERMS, ROWS, LANES)] * 2,
        in_specs=[HBM] * BANDS,
        out_specs=[HBM] * 2,
        scratch_shapes=[pltpu.VMEM((2, TERMS, ROWS, LANES), F32), dma(BANDS)],
        compiler_params=pltpu.CompilerParams(vmem_limit_bytes=VMEM_BYTES),
        cost_estimate=WEIGHT,
        name="faces",
    )(*pieces)


def start_all(pairs, sems):
    copies = [pltpu.make_async_copy(a, b, sems.at[n]) for n, (a, b) in enumerate(pairs)]
    for c in copies:
        c.start()
    return copies


def weigh(cond, w, planes, scale):
    for p in planes:
        w[p, 0] = scale * cond[0, p]
        for k in range(DIM):
            for n in range(DEG):
                w[p, 1 + DEG * k + n] = (scale * MEANS[n]) * cond[k + 1, p]


def laplace_plane(v, lap, p, zero, up_row, dn_row):
    lane = lax.broadcasted_iota(jnp.int32, (ROWS, LANES), 1)
    first_lane, last_lane = lane == 0, lane == LANES - 1
    rows = pl.ds(TOP, ROWS)

    def group(t, carry):
        for jj in range(T4):
            j = t * T4 + jj
            v[j, p + 1, pl.ds(TOP - 1, 1), :] = up_row(t, p, jj)
            v[j, p + 1, pl.ds(TOP + ROWS, 1), :] = dn_row(t, p, jj)
        for jj in range(T4):
            j = t * T4 + jj
            c = v[j, p + 1, rows, :]
            up = v[j, p + 1, pl.ds(zero + (TOP - 1), ROWS), :]
            dn = v[j, p + 1, pl.ds(zero + (TOP + 1), ROWS), :]
            right = jnp.where(last_lane, 0.0, pltpu.roll(c, LANES - 1, 1))
            left = jnp.where(first_lane, 0.0, pltpu.roll(c, 1, 1))
            beside = v[j, p + 2, rows, :] + v[j, p, rows, :]
            beside = beside + dn + up
            beside = beside + right + left
            lap[j] = 6.0 * c - beside
        return carry

    lax.fori_loop(0, 4, group, 0)


def couple_plane(lap, w, p, emit):
    for half in range(2):
        rows = pl.ds(8 * half, 8)
        weights = [w[p, m, rows, :] for m in range(1 + DEG * DIM)]
        for i in range(TERMS):
            acc = weights[0] * lap[i, rows, :]
            for j, k, n in COUPLE[i]:
                acc = acc + weights[DEG * k + n] * lap[j, rows, :]
            emit(i, half, acc)


def waiting(groups, sems):
    at, held_back = 0, []
    for pairs in groups:
        copies = []
        for a, b in pairs:
            copies.append(pltpu.make_async_copy(a, b, sems.at[at]))
            at += 1
        for c in copies:
            c.start()
        held_back.append(copies)
    return held_back


def place_of(s_ref, k):
    h = jnp.bitwise_xor(s_ref[0], k >> 2)
    t = jnp.bitwise_xor(s_ref[1], k & 3)
    return h, t


def conductivity_pairs(s_ref, near, far, cond):
    odd = s_ref[2]
    return [
        (near, cond.at[:, pl.ds(2 * odd, 2)]),
        (far, cond.at[:, pl.ds(2 * (1 - odd), 2)]),
    ]


def first_kernel(edge, s_ref, *refs):
    outer, inner, near, far = refs[0:8], refs[8], refs[9], refs[10]
    if edge:
        zlo, zhi = refs[11:13]
        sol, y0, y15, z0, z3 = refs[15:20]
        scratch = refs[20:]
    else:
        sol, y0, y15 = refs[11:14]
        scratch = refs[14:]
    v, halo, lap, out, cond, w, y0v, y15v, sem_v, sem_o, sem_e = scratch
    h, zero = s_ref[0], s_ref[3]
    planes = (0, 3) if edge else (1, 2)
    rows = pl.ds(TOP, ROWS)

    early = conductivity_pairs(s_ref, near, far, cond)
    late = []
    for n in range(8):
        hk, tk = n // 4, n % 4
        group = late if edge and hk == 1 else early
        group.append((inner.at[n, pl.ds(0, T4)], v.at[pl.ds(tk * T4, T4), 2 + hk, rows]))
        if not edge:
            early.append((inner.at[n, pl.ds(T4, 3)], halo.at[tk, 1 + hk]))
        hk, tk = place_of(s_ref, n)
        early.append((outer[n].at[pl.ds(0, T4)], v.at[pl.ds(tk * T4, T4), 3 * hk + 1, rows]))
        if edge:
            early.append((outer[n].at[pl.ds(T4, 3)], halo.at[tk, 3 * hk]))
    if edge:
        for k in range(4):
            _, tk = place_of(s_ref, k)
            terms = pl.ds(tk * T4, T4)
            early.append((zlo.at[pl.ds(k * T4, T4)], v.at[terms, 5 * (1 - h), rows]))
            early.append((zhi.at[pl.ds(k * T4, T4)], v.at[terms, 5 * h, rows]))
    early, late = waiting([early, late], sem_v)
    for t in range(4):
        for n in planes:
            y0v[t, n, T4:24, :] = jnp.zeros((24 - T4, LANES), F32)
            y15v[t, n, T4:24, :] = jnp.zeros((24 - T4, LANES), F32)
    for c in early:
        c.wait()
    weigh(cond, w, planes, MIX)

    def up_row(t, p, jj):
        return halo[t, p, jj // 16, pl.ds(jj % 16, 1), :]

    def dn_row(t, p, jj):
        return halo[t, p, (24 + jj) // 16, pl.ds((24 + jj) % 16, 1), :]

    def plane_step(n, carry):
        @pl.when(n == 1)
        def _():
            for c in late:
                c.wait()

        p = planes[0] + (planes[1] - planes[0]) * n
        laplace_plane(v, lap, p, zero, up_row, dn_row)

        def emit(i, half, acc):
            value = KEEP * v[i, p + 1, pl.ds(TOP + 8 * half, 8), :] + acc
            out[i, p, pl.ds(8 * half, 8), :] = value
            if half == 0:
                y0v[i // T4, p, pl.ds(i % T4, 1), :] = value[0:1]
            else:
                y15v[i // T4, p, pl.ds(i % T4, 1), :] = value[7:8]

        couple_plane(lap, w, p, emit)
        for c in sends(out, sol, sem_o, p):
            c.start()
        if edge:
            for m in range(2):

                @pl.when(n == m)
                def _():
                    face(m).start()

        return carry

    def face(m):
        return pltpu.make_async_copy(out.at[:, planes[m]], (z0, z3)[m], sem_e.at[4 + m])

    lax.fori_loop(0, 2, plane_step, 0)
    ends = [(a.at[:, p], b.at[:, p]) for p in planes for a, b in ((y0v, y0), (y15v, y15))]
    ends = start_all(ends, sem_e)
    if edge:
        ends += [face(0), face(1)]
    for c in ends:
        c.wait()
    for p in planes:
        for c in sends(out, sol, sem_o, p):
            c.wait()


def sends(out, to, sem, p):
    half = p // 2
    return [
        pltpu.make_async_copy(
            out.at[pl.ds(t * T4, T4), p], to.at[half * 4 + t], sem.at[p * 4 + t]
        )
        for t in range(4)
    ]


def second_kernel(s_ref, *refs):
    outer, (inner, middle, edge, below, above, yup, ydn, near, far) = refs[0:8], refs[8:17]
    outs = refs[17:25]
    v, r, lap, out, cond, w, upv, dnv, sem_v, sem_o = refs[25:]
    h, zero = s_ref[0], s_ref[3]
    rows = pl.ds(TOP, ROWS)

    groups = [[(yup, upv), (ydn, dnv), (below, v.at[:, 0, rows])], [], [], []]
    groups[0] += conductivity_pairs(s_ref, near, far, cond)
    for n in range(8):
        hk, tk = n // 4, n % 4
        terms = pl.ds(tk * T4, T4)
        groups[hk].append((middle.at[n], v.at[terms, 2 + hk, rows]))
        groups[2 * hk].append((edge.at[n], v.at[terms, 1 + 3 * hk, rows]))
        groups[hk].append((inner.at[n, pl.ds(0, T4)], r.at[terms, 1 + hk]))
        hk, tk = place_of(s_ref, n)
        groups[0].append((outer[n].at[pl.ds(0, T4)], r.at[pl.ds(tk * T4, T4), 3 * hk]))
    groups[3].append((above, v.at[:, 5, rows]))
    groups = waiting(groups, sem_v)
    for c in groups[0]:
        c.wait()
    weigh(cond, w, range(4), -1.0)

    def up_row(t, p, jj):
        return upv[t, p, pl.ds(jj, 1), :]

    def dn_row(t, p, jj):
        return dnv[t, p, pl.ds(jj, 1), :]

    def scattered(group):
        result = []
        for kk in range(4):
            k = group * 4 + kk
            hk, tk = place_of(s_ref, k)
            result.append(
                pltpu.make_async_copy(
                    out.at[pl.ds(tk * T4, T4), pl.ds(2 * hk, 2)], outs[k], sem_o.at[k]
                )
            )
        return result

    def plane_step(p, carry):
        for m in range(1, 4):

            @pl.when(p == m)
            def _():
                for c in groups[m]:
                    c.wait()

        laplace_plane(v, lap, p, zero, up_row, dn_row)

        def emit(i, half, acc):
            own = pl.ds(8 * half, 8)
            out[i, p, own, :] = r[i, p, own, :] + acc

        couple_plane(lap, w, p, emit)
        for group in range(2):

            @pl.when((p % 2 == 1) & (jnp.bitwise_xor(h, group) == p // 2))
            def _():
                for c in scattered(group):
                    c.start()

        return carry

    lax.fori_loop(0, 4, plane_step, 0)
    for c in scattered(0) + scattered(1):
        c.wait()


TOP = 8
PIECE = held(T4, 2, ROWS, LANES)
PIECES = held(BANDS, T4, ROWS, LANES)
FACE = held(TERMS, ROWS, LANES)
EDGE = held(4, 4, 24, LANES)
RES_SHAPES = [PIECE] * 8


def first(edge, info, *arrays):
    return pl.pallas_call(
        functools.partial(first_kernel, edge),
        out_shape=[PIECES, EDGE, EDGE] + ([FACE, FACE] if edge else []),
        in_specs=[SMEM] + [HBM] * len(arrays),
        out_specs=[HBM] * (5 if edge else 3),
        scratch_shapes=[
            pltpu.VMEM((TERMS, 6, 32, LANES), F32),
            pltpu.VMEM((4, 4, 3, ROWS, LANES), F32),
            pltpu.VMEM((TERMS, ROWS, LANES), F32),
            pltpu.VMEM((TERMS, 4, ROWS, LANES), F32),
            pltpu.VMEM((DIM + 1, 4, ROWS, LANES), F32),
            pltpu.VMEM((4, 1 + DEG * DIM, ROWS, LANES), F32),
            pltpu.VMEM((4, 4, 24, LANES), F32),
            pltpu.VMEM((4, 4, 24, LANES), F32),
            dma(34), dma(16), dma(6),
        ],
        compiler_params=pltpu.CompilerParams(vmem_limit_bytes=VMEM_BYTES),
        input_output_aliases={14: 1, 15: 2} if edge else {},
        cost_estimate=None if edge else pl.CostEstimate(flops=10**10, transcendentals=0, bytes_accessed=10**7),
        name="first_edge" if edge else "first_middle",
    )(info, *arrays)


def second(info, *arrays):
    return pl.pallas_call(
        second_kernel,
        out_shape=RES_SHAPES,
        in_specs=[SMEM] + [HBM] * 17,
        out_specs=[HBM] * len(RES_SHAPES),
        scratch_shapes=[
            pltpu.VMEM((TERMS, 6, 32, LANES), F32),
            pltpu.VMEM((TERMS, 4, ROWS, LANES), F32),
            pltpu.VMEM((TERMS, ROWS, LANES), F32),
            pltpu.VMEM((TERMS, 4, ROWS, LANES), F32),
            pltpu.VMEM((DIM + 1, 4, ROWS, LANES), F32),
            pltpu.VMEM((4, 1 + DEG * DIM, ROWS, LANES), F32),
            pltpu.VMEM((4, 4, 24, LANES), F32),
            pltpu.VMEM((4, 4, 24, LANES), F32),
            dma(38), dma(8),
        ],
        compiler_params=pltpu.CompilerParams(vmem_limit_bytes=VMEM_BYTES),
        cost_estimate=WEIGHT,
        name="second",
    )(info, *arrays)


BAND = ("half", "term")
ORDER = (4, 2, 6, 5, 3, 7, 1)


def swapped(pieces):
    return lax.all_to_all(pieces, BAND, 0, 0, tiled=True)


def exchange(pieces):
    got = [None] * 8
    got[0] = pieces[0]
    for k in ORDER:
        got[k] = lax.ppermute(pieces[k], BAND, [(i, i ^ k) for i in range(8)])
    return got


def unpacked(got, band, other):
    whole = jnp.zeros((T4, 2, 128, LANES), F32)
    for n, k in enumerate((0,) + ORDER):
        if n == 5:
            whole, other = lax.optimization_barrier((whole, other))
        start = jnp.bitwise_xor(band, k) * ROWS
        whole = lax.dynamic_update_slice(whole, got[k], (0, 0, start, 0))
    return whole, other


def joined(pieces):
    return jnp.transpose(pieces, (1, 0, 2, 3)).reshape(T4, 128, LANES)


def shards(right_side, mean_cond, cond_terms):
    quads = lax.axis_size("quad")
    band = lax.axis_index(BAND)
    h, t = band // 4, band % 4
    info = jnp.stack([h, t, band % 2, 0 * band]).astype(jnp.int32)
    up = [(i, i + 1) for i in range(quads - 1)]
    down = [(i + 1, i) for i in range(quads - 1)]

    outer = exchange(pack(True, info, right_side))
    inner = pack(False, info, right_side)[0]
    inner = swapped(inner)

    def z_shift(face, lower_half):
        pairs = []
        for q in range(quads):
            for b in range(BANDS):
                other = q - 1 if (b // 4) == lower_half else q + 1
                if 0 <= other < quads:
                    pairs.append((q * BANDS + b, other * BANDS + b))
        return lax.ppermute(face, ("quad",) + BAND, pairs)

    low, high = faces(*outer)
    zlo = z_shift(low, 0)
    zhi = z_shift(high, 1)

    local = jnp.concatenate([mean_cond[None], cond_terms], axis=0)
    own = lax.dynamic_slice_in_dim(local, h * ROWS, ROWS, axis=2)
    rest = lax.dynamic_slice_in_dim(local, (1 - h) * ROWS, ROWS, axis=2)
    near = lax.ppermute(own, BAND, [(4 * a + b, 2 * b + a) for a in range(2) for b in range(4)])
    far = lax.ppermute(rest, BAND, [(4 * a + b, 2 * b + 1 - a) for a in range(2) for b in range(4)])

    sol_middle, y0, y15 = first(False, info, *outer, inner, near, far)
    sol_edge, y0, y15, z0, z3 = first(True, info, *outer, inner, near, far, zlo, zhi, y0, y15)

    below = lax.ppermute(z3, "quad", up)
    above = lax.ppermute(z0, "quad", down)
    yup = lax.ppermute(y15, BAND, [(i, i + 1) for i in range(7)])
    ydn = lax.ppermute(y0, BAND, [(i + 1, i) for i in range(7)])

    solution = jnp.zeros((T4, 2, 128, LANES), F32)
    for plane, part in ((1 - h, swapped(sol_middle)), (h, swapped(sol_edge))):
        solution = lax.dynamic_update_slice(solution, joined(part)[:, None], (0, plane, 0, 0))
    res = second(
        info, *outer, inner, fixed(sol_middle), fixed(sol_edge), below, above, yup, ydn, near, far
    )
    residual, solution = unpacked(exchange(res), band, solution)
    return (solution, residual)


def solution(mesh):
    grid = Mesh(mesh.devices.reshape(-1, 2, 4), ("quad", "half", "term"))
    field = P("term", ("quad", "half"), None, None)
    return jax.shard_map(
        shards,
        mesh=grid,
        in_specs=(field, P(("quad", "half"), "term", None), P(None, ("quad", "half"), "term", None)),
        out_specs=(field, field),
        check_vma=False,
    )
```

```python
import functools
import math

import jax
import jax.numpy as jnp
from jax import lax
from jax.experimental import pallas as pl
from jax.experimental.pallas import tpu as pltpu
from jax.sharding import Mesh, PartitionSpec as P

DIM = 6
DEG = 3
LOWER = 2.0
UPPER = 72.0

TERMS = 84
T4 = 21
ROWS = 16
LANES = 128
F32 = jnp.float32
WEIGHT = pl.CostEstimate(flops=10**12, transcendentals=0, bytes_accessed=10**9)
VMEM_BYTES = 20 * 1024 * 1024


def compositions(degree_sum, slots_left):
    if slots_left == 1:
        return [[degree_sum]]
    listing = []
    for leading in range(degree_sum, -1, -1):
        for remainder in compositions(degree_sum - leading, slots_left - 1):
            listing.append([leading] + remainder)
    return listing


def couplings(variables, degree):
    indices = []
    for level in range(degree + 1):
        indices.extend(compositions(level, variables))
    place = {tuple(m): n for n, m in enumerate(indices)}
    result = []
    for first in indices:
        found = []
        for k in range(variables):
            for step in (-1, 1):
                other = list(first)
                other[k] += step
                j = place.get(tuple(other))
                if j is not None:
                    found.append((j, k, max(first[k], other[k])))
        result.append(found)
    return result


def scalars():
    center = 0.5 * (UPPER + LOWER)
    half = 0.5 * (UPPER - LOWER)
    sigma = center / half
    rho0 = 1.0 / sigma
    rho1 = 1.0 / (2.0 * sigma - rho0)
    keep = (1.0 + rho1 * rho0) / center + 2.0 * rho1 / half
    mix = -2.0 * rho1 / half / center
    return keep, mix


COUPLE = couplings(DIM, DEG)
MEANS = [n / math.sqrt(4.0 * n * n - 1.0) for n in range(1, DEG + 1)]
KEEP, MIX = scalars()

HBM = pl.BlockSpec(memory_space=pltpu.HBM)
SMEM = pl.BlockSpec(memory_space=pltpu.SMEM)
BANDS = 8


def held(*shape):
    return pltpu.HBM(shape, F32)


def fixed(array):
    return pltpu.with_memory_space_constraint(array, pltpu.HBM)


def dma(count):
    return pltpu.SemaphoreType.DMA((count,))


def pack_kernel(s_ref, x_ref, *refs):
    outer, inner = refs[:BANDS], refs[BANDS]
    xv, hv, sem_in, sem_main, sem_halo = refs[BANDS + 1 :]
    h = s_ref[0]
    band = 4 * h + s_ref[1]
    loads = start_all([(x_ref.at[:, h], xv.at[0]), (x_ref.at[:, 1 - h], xv.at[1])], sem_in)
    copies = []
    for n in range(2):
        loads[n].wait()
        places = []
        for k in range(BANDS):
            if n == 0:
                d, out = jnp.bitwise_xor(band, k), outer[k]
                rows = pl.ds(pl.multiple_of(d * ROWS, ROWS), ROWS)
                above = jnp.maximum(d * ROWS - 1, 0)
                below = jnp.minimum(d * ROWS + ROWS, 127)
            else:
                d, out = k, inner.at[k]
                rows = pl.ds(d * ROWS, ROWS)
                above, below = max(d * ROWS - 1, 0), min(d * ROWS + ROWS, 127)
            places.append((d, out, above, below))
            c = pltpu.make_async_copy(
                xv.at[n, :, rows, :], out.at[pl.ds(0, T4)], sem_main.at[n * BANDS + k]
            )
            c.start()
            copies.append(c)
        for k, (d, out, above, below) in enumerate(places):
            for j in range(T4):
                up = xv[n, j, pl.ds(above, 1), :]
                dn = xv[n, j, pl.ds(below, 1), :]
                up = jnp.where(d == 0, jnp.zeros_like(up), up)
                dn = jnp.where(d == BANDS - 1, jnp.zeros_like(dn), dn)
                a, b = j, 24 + j
                hv[n, k, a // 16, pl.ds(a % 16, 1), :] = up
                hv[n, k, b // 16, pl.ds(b % 16, 1), :] = dn
            c = pltpu.make_async_copy(
                hv.at[n, k], out.at[pl.ds(T4, 3)], sem_halo.at[n * BANDS + k]
            )
            c.start()
            copies.append(c)
    for c in copies:
        c.wait()


def pack(info, x):
    return pl.pallas_call(
        pack_kernel,
        out_shape=[held(24, ROWS, LANES)] * BANDS + [held(BANDS, 24, ROWS, LANES)],
        in_specs=[SMEM, HBM],
        out_specs=[HBM] * (BANDS + 1),
        scratch_shapes=[
            pltpu.VMEM((2, T4, 128, LANES), F32),
            pltpu.VMEM((2, BANDS, 3, ROWS, LANES), F32),
            dma(2), dma(16), dma(16),
        ],
        compiler_params=pltpu.CompilerParams(vmem_limit_bytes=VMEM_BYTES),
        name="pack",
    )(info, fixed(x))


def faces_kernel(*refs):
    pieces, faces, (held_v, sems) = refs[:BANDS], refs[BANDS : BANDS + 2], refs[BANDS + 2 :]
    loads = start_all(
        [
            (pieces[k].at[pl.ds(0, T4)], held_v.at[k // 4, pl.ds(k % 4 * T4, T4)])
            for k in range(BANDS)
        ],
        sems,
    )
    for c in loads:
        c.wait()
    stores = start_all([(held_v.at[n], faces[n]) for n in range(2)], sems)
    for c in stores:
        c.wait()


def faces(*pieces):
    return pl.pallas_call(
        faces_kernel,
        out_shape=[held(TERMS, ROWS, LANES)] * 2,
        in_specs=[HBM] * BANDS,
        out_specs=[HBM] * 2,
        scratch_shapes=[pltpu.VMEM((2, TERMS, ROWS, LANES), F32), dma(BANDS)],
        compiler_params=pltpu.CompilerParams(vmem_limit_bytes=VMEM_BYTES),
        cost_estimate=WEIGHT,
        name="faces",
    )(*pieces)


def start_all(pairs, sems):
    copies = [pltpu.make_async_copy(a, b, sems.at[n]) for n, (a, b) in enumerate(pairs)]
    for c in copies:
        c.start()
    return copies


def weigh(cond, w, planes, scale):
    for p in planes:
        w[p, 0] = scale * cond[0, p]
        for k in range(DIM):
            for n in range(DEG):
                w[p, 1 + DEG * k + n] = (scale * MEANS[n]) * cond[k + 1, p]


def laplace_plane(v, lap, p, zero, up_row, dn_row):
    lane = lax.broadcasted_iota(jnp.int32, (ROWS, LANES), 1)
    first_lane, last_lane = lane == 0, lane == LANES - 1
    rows = pl.ds(TOP, ROWS)

    def group(t, carry):
        for jj in range(T4):
            j = t * T4 + jj
            v[j, p + 1, pl.ds(TOP - 1, 1), :] = up_row(t, p, jj)
            v[j, p + 1, pl.ds(TOP + ROWS, 1), :] = dn_row(t, p, jj)
        for jj in range(T4):
            j = t * T4 + jj
            c = v[j, p + 1, rows, :]
            up = v[j, p + 1, pl.ds(zero + (TOP - 1), ROWS), :]
            dn = v[j, p + 1, pl.ds(zero + (TOP + 1), ROWS), :]
            right = jnp.where(last_lane, 0.0, pltpu.roll(c, LANES - 1, 1))
            left = jnp.where(first_lane, 0.0, pltpu.roll(c, 1, 1))
            beside = v[j, p + 2, rows, :] + v[j, p, rows, :]
            beside = beside + dn + up
            beside = beside + right + left
            lap[j] = 6.0 * c - beside
        return carry

    lax.fori_loop(0, 4, group, 0)


def couple_plane(lap, w, p, emit):
    for half in range(2):
        rows = pl.ds(8 * half, 8)
        weights = [w[p, m, rows, :] for m in range(1 + DEG * DIM)]
        for i in range(TERMS):
            acc = weights[0] * lap[i, rows, :]
            for j, k, n in COUPLE[i]:
                acc = acc + weights[DEG * k + n] * lap[j, rows, :]
            emit(i, half, acc)


def waiting(groups, sems):
    at, held_back = 0, []
    for pairs in groups:
        copies = []
        for a, b in pairs:
            copies.append(pltpu.make_async_copy(a, b, sems.at[at]))
            at += 1
        for c in copies:
            c.start()
        held_back.append(copies)
    return held_back


def place_of(s_ref, k):
    h = jnp.bitwise_xor(s_ref[0], k >> 2)
    t = jnp.bitwise_xor(s_ref[1], k & 3)
    return h, t


def conductivity_pairs(s_ref, near, far, cond):
    odd = s_ref[2]
    return [
        (near, cond.at[:, pl.ds(2 * odd, 2)]),
        (far, cond.at[:, pl.ds(2 * (1 - odd), 2)]),
    ]


def first_kernel(edge, s_ref, *refs):
    outer, inner, near, far = refs[0:8], refs[8], refs[9], refs[10]
    if edge:
        zlo, zhi = refs[11:13]
        sol, y0, y15, z0, z3 = refs[15:20]
        scratch = refs[20:]
    else:
        sol, y0, y15 = refs[11:14]
        scratch = refs[14:]
    v, halo, lap, out, cond, w, y0v, y15v, sem_v, sem_o, sem_e = scratch
    h, zero = s_ref[0], s_ref[3]
    planes = (0, 3) if edge else (1, 2)
    rows = pl.ds(TOP, ROWS)

    early = conductivity_pairs(s_ref, near, far, cond)
    late = []
    for n in range(8):
        hk, tk = n // 4, n % 4
        group = late if edge and hk == 1 else early
        group.append((inner.at[n, pl.ds(0, T4)], v.at[pl.ds(tk * T4, T4), 2 + hk, rows]))
        if not edge:
            early.append((inner.at[n, pl.ds(T4, 3)], halo.at[tk, 1 + hk]))
        hk, tk = place_of(s_ref, n)
        early.append((outer[n].at[pl.ds(0, T4)], v.at[pl.ds(tk * T4, T4), 3 * hk + 1, rows]))
        if edge:
            early.append((outer[n].at[pl.ds(T4, 3)], halo.at[tk, 3 * hk]))
    if edge:
        for k in range(4):
            _, tk = place_of(s_ref, k)
            terms = pl.ds(tk * T4, T4)
            early.append((zlo.at[pl.ds(k * T4, T4)], v.at[terms, 5 * (1 - h), rows]))
            early.append((zhi.at[pl.ds(k * T4, T4)], v.at[terms, 5 * h, rows]))
    early, late = waiting([early, late], sem_v)
    for t in range(4):
        for n in planes:
            y0v[t, n, T4:24, :] = jnp.zeros((24 - T4, LANES), F32)
            y15v[t, n, T4:24, :] = jnp.zeros((24 - T4, LANES), F32)
    for c in early:
        c.wait()
    weigh(cond, w, planes, MIX)

    def up_row(t, p, jj):
        return halo[t, p, jj // 16, pl.ds(jj % 16, 1), :]

    def dn_row(t, p, jj):
        return halo[t, p, (24 + jj) // 16, pl.ds((24 + jj) % 16, 1), :]

    def plane_step(n, carry):
        @pl.when(n == 1)
        def _():
            for c in late:
                c.wait()

        p = planes[0] + (planes[1] - planes[0]) * n
        laplace_plane(v, lap, p, zero, up_row, dn_row)

        def emit(i, half, acc):
            value = KEEP * v[i, p + 1, pl.ds(TOP + 8 * half, 8), :] + acc
            out[i, p, pl.ds(8 * half, 8), :] = value
            if half == 0:
                y0v[i // T4, p, pl.ds(i % T4, 1), :] = value[0:1]
            else:
                y15v[i // T4, p, pl.ds(i % T4, 1), :] = value[7:8]

        couple_plane(lap, w, p, emit)
        for c in sends(out, sol, sem_o, p):
            c.start()
        if edge:
            for m in range(2):

                @pl.when(n == m)
                def _():
                    face(m).start()

        return carry

    def face(m):
        return pltpu.make_async_copy(out.at[:, planes[m]], (z0, z3)[m], sem_e.at[4 + m])

    lax.fori_loop(0, 2, plane_step, 0)
    ends = [(a.at[:, p], b.at[:, p]) for p in planes for a, b in ((y0v, y0), (y15v, y15))]
    ends = start_all(ends, sem_e)
    if edge:
        ends += [face(0), face(1)]
    for c in ends:
        c.wait()
    for p in planes:
        for c in sends(out, sol, sem_o, p):
            c.wait()


def sends(out, to, sem, p):
    half = p // 2
    return [
        pltpu.make_async_copy(
            out.at[pl.ds(t * T4, T4), p], to.at[half * 4 + t], sem.at[p * 4 + t]
        )
        for t in range(4)
    ]


def second_kernel(s_ref, *refs):
    outer, (inner, middle, edge, below, above, yup, ydn, near, far) = refs[0:8], refs[8:17]
    outs = refs[17:25]
    v, r, lap, out, cond, w, upv, dnv, sem_v, sem_o = refs[25:]
    h, zero = s_ref[0], s_ref[3]
    rows = pl.ds(TOP, ROWS)

    groups = [[(yup, upv), (ydn, dnv), (below, v.at[:, 0, rows])], [], [], []]
    groups[0] += conductivity_pairs(s_ref, near, far, cond)
    for n in range(8):
        hk, tk = n // 4, n % 4
        terms = pl.ds(tk * T4, T4)
        groups[hk].append((middle.at[n], v.at[terms, 2 + hk, rows]))
        groups[2 * hk].append((edge.at[n], v.at[terms, 1 + 3 * hk, rows]))
        groups[hk].append((inner.at[n, pl.ds(0, T4)], r.at[terms, 1 + hk]))
        hk, tk = place_of(s_ref, n)
        groups[0].append((outer[n].at[pl.ds(0, T4)], r.at[pl.ds(tk * T4, T4), 3 * hk]))
    groups[3].append((above, v.at[:, 5, rows]))
    groups = waiting(groups, sem_v)
    for c in groups[0]:
        c.wait()
    weigh(cond, w, range(4), -1.0)

    def up_row(t, p, jj):
        return upv[t, p, pl.ds(jj, 1), :]

    def dn_row(t, p, jj):
        return dnv[t, p, pl.ds(jj, 1), :]

    def scattered(group):
        result = []
        for kk in range(4):
            k = group * 4 + kk
            hk, tk = place_of(s_ref, k)
            result.append(
                pltpu.make_async_copy(
                    out.at[pl.ds(tk * T4, T4), pl.ds(2 * hk, 2)], outs[k], sem_o.at[k]
                )
            )
        return result

    def plane_step(p, carry):
        for m in range(1, 4):

            @pl.when(p == m)
            def _():
                for c in groups[m]:
                    c.wait()

        laplace_plane(v, lap, p, zero, up_row, dn_row)

        def emit(i, half, acc):
            own = pl.ds(8 * half, 8)
            out[i, p, own, :] = r[i, p, own, :] + acc

        couple_plane(lap, w, p, emit)
        for group in range(2):

            @pl.when((p % 2 == 1) & (jnp.bitwise_xor(h, group) == p // 2))
            def _():
                for c in scattered(group):
                    c.start()

        return carry

    lax.fori_loop(0, 4, plane_step, 0)
    for c in scattered(0) + scattered(1):
        c.wait()


TOP = 8
PIECE = held(T4, 2, ROWS, LANES)
PIECES = held(BANDS, T4, ROWS, LANES)
FACE = held(TERMS, ROWS, LANES)
EDGE = held(4, 4, 24, LANES)
RES_SHAPES = [PIECE] * 8


def first(edge, info, *arrays):
    return pl.pallas_call(
        functools.partial(first_kernel, edge),
        out_shape=[PIECES, EDGE, EDGE] + ([FACE, FACE] if edge else []),
        in_specs=[SMEM] + [HBM] * len(arrays),
        out_specs=[HBM] * (5 if edge else 3),
        scratch_shapes=[
            pltpu.VMEM((TERMS, 6, 32, LANES), F32),
            pltpu.VMEM((4, 4, 3, ROWS, LANES), F32),
            pltpu.VMEM((TERMS, ROWS, LANES), F32),
            pltpu.VMEM((TERMS, 4, ROWS, LANES), F32),
            pltpu.VMEM((DIM + 1, 4, ROWS, LANES), F32),
            pltpu.VMEM((4, 1 + DEG * DIM, ROWS, LANES), F32),
            pltpu.VMEM((4, 4, 24, LANES), F32),
            pltpu.VMEM((4, 4, 24, LANES), F32),
            dma(34), dma(16), dma(6),
        ],
        compiler_params=pltpu.CompilerParams(vmem_limit_bytes=VMEM_BYTES),
        input_output_aliases={14: 1, 15: 2} if edge else {},
        cost_estimate=None if edge else pl.CostEstimate(flops=10**10, transcendentals=0, bytes_accessed=10**7),
        name="first_edge" if edge else "first_middle",
    )(info, *arrays)


def second(info, *arrays):
    return pl.pallas_call(
        second_kernel,
        out_shape=RES_SHAPES,
        in_specs=[SMEM] + [HBM] * 17,
        out_specs=[HBM] * len(RES_SHAPES),
        scratch_shapes=[
            pltpu.VMEM((TERMS, 6, 32, LANES), F32),
            pltpu.VMEM((TERMS, 4, ROWS, LANES), F32),
            pltpu.VMEM((TERMS, ROWS, LANES), F32),
            pltpu.VMEM((TERMS, 4, ROWS, LANES), F32),
            pltpu.VMEM((DIM + 1, 4, ROWS, LANES), F32),
            pltpu.VMEM((4, 1 + DEG * DIM, ROWS, LANES), F32),
            pltpu.VMEM((4, 4, 24, LANES), F32),
            pltpu.VMEM((4, 4, 24, LANES), F32),
            dma(38), dma(8),
        ],
        compiler_params=pltpu.CompilerParams(vmem_limit_bytes=VMEM_BYTES),
        cost_estimate=WEIGHT,
        name="second",
    )(info, *arrays)


BAND = ("half", "term")
ORDER = (4, 2, 6, 5, 3, 7, 1)


def swapped(pieces):
    return lax.all_to_all(pieces, BAND, 0, 0, tiled=True)


def exchange(pieces):
    got = [None] * 8
    got[0] = pieces[0]
    for k in ORDER:
        got[k] = lax.ppermute(pieces[k], BAND, [(i, i ^ k) for i in range(8)])
    return got


def unpacked(got, band, other):
    whole = jnp.zeros((T4, 2, 128, LANES), F32)
    for n, k in enumerate((0,) + ORDER):
        if n == 5:
            whole, other = lax.optimization_barrier((whole, other))
        start = jnp.bitwise_xor(band, k) * ROWS
        whole = lax.dynamic_update_slice(whole, got[k], (0, 0, start, 0))
    return whole, other


def joined(pieces):
    return jnp.transpose(pieces, (1, 0, 2, 3)).reshape(T4, 128, LANES)


def shards(right_side, mean_cond, cond_terms):
    quads = lax.axis_size("quad")
    band = lax.axis_index(BAND)
    h, t = band // 4, band % 4
    info = jnp.stack([h, t, band % 2, 0 * band]).astype(jnp.int32)
    up = [(i, i + 1) for i in range(quads - 1)]
    down = [(i + 1, i) for i in range(quads - 1)]

    *outer, inner = pack(info, right_side)
    outer = exchange(outer)
    inner = swapped(inner)

    def z_shift(face, lower_half):
        pairs = []
        for q in range(quads):
            for b in range(BANDS):
                other = q - 1 if (b // 4) == lower_half else q + 1
                if 0 <= other < quads:
                    pairs.append((q * BANDS + b, other * BANDS + b))
        return lax.ppermute(face, ("quad",) + BAND, pairs)

    low, high = faces(*outer)
    zlo = z_shift(low, 0)
    zhi = z_shift(high, 1)

    local = jnp.concatenate([mean_cond[None], cond_terms], axis=0)
    own = lax.dynamic_slice_in_dim(local, h * ROWS, ROWS, axis=2)
    rest = lax.dynamic_slice_in_dim(local, (1 - h) * ROWS, ROWS, axis=2)
    near = lax.ppermute(own, BAND, [(4 * a + b, 2 * b + a) for a in range(2) for b in range(4)])
    far = lax.ppermute(rest, BAND, [(4 * a + b, 2 * b + 1 - a) for a in range(2) for b in range(4)])

    sol_middle, y0, y15 = first(False, info, *outer, inner, near, far)
    sol_edge, y0, y15, z0, z3 = first(True, info, *outer, inner, near, far, zlo, zhi, y0, y15)

    below = lax.ppermute(z3, "quad", up)
    above = lax.ppermute(z0, "quad", down)
    yup = lax.ppermute(y15, BAND, [(i, i + 1) for i in range(7)])
    ydn = lax.ppermute(y0, BAND, [(i + 1, i) for i in range(7)])

    solution = jnp.zeros((T4, 2, 128, LANES), F32)
    for plane, part in ((1 - h, swapped(sol_middle)), (h, swapped(sol_edge))):
        solution = lax.dynamic_update_slice(solution, joined(part)[:, None], (0, plane, 0, 0))
    res = second(
        info, *outer, inner, fixed(sol_middle), fixed(sol_edge), below, above, yup, ydn, near, far
    )
    residual, solution = unpacked(exchange(res), band, solution)
    return (solution, residual)


def solution(mesh):
    grid = Mesh(mesh.devices.reshape(-1, 2, 4), ("quad", "half", "term"))
    field = P("term", ("quad", "half"), None, None)
    return jax.shard_map(
        shards,
        mesh=grid,
        in_specs=(field, P(("quad", "half"), "term", None), P(None, ("quad", "half"), "term", None)),
        out_specs=(field, field),
        check_vma=False,
    )
```
